768 devices in a mesh: cond: 16 (over x, y_lo, core), slab: 48 (over z, y_hi).
Axes of the slice: x: 4, y: 8 (y_hi: 4, y_lo: 2; y = y_hi * 2 + y_lo), z: 12, core: 2. Of those that a mesh axis runs over, the one named last changes fastest.
Arguments:
- adjoint: float32 [16, 192, 512, 128], P('cond', 'slab'), may hold values from -6 to 6
- phase: bfloat16 [16, 192, 512, 128], P('cond', 'slab'), may hold values from -1.09375 to 1.09375
- targets: bfloat16 [16, 1536, 128], P('cond', 'slab'), may hold values from -1 to 1
- owners: int32 [16, 1536, 1], P('cond', 'slab'), may hold values from 0 to 47; in each aligned block of 32 rows (0 to 31, 32 to 63, ..., all dimensions but the last counted through in order) at most 2 rows name the same one
- target_cell: int32 [16, 1536], P('cond', 'slab'), may hold values from 0 to 2047
- rate_index: int32 [16], P('cond'), may hold values from 0 to 7
- inflow_rates: float32 [8], replicated, may hold values from 0.5 to 2
- wall_mask: int32 [2, 192, 512], P(None, 'slab'), may hold values 0 or 1
Outputs:
- adjoint_out: float32 [16, 192, 512, 128], P('cond', 'slab')
- wall_gradient: float32 [2, 192, 512], P(None, 'slab')
The draws below stay inside these ranges and needn't reach their ends.
Inputs may be any that keep to these rules, and one draw needn't show every extreme that they name: `owners`: within each aligned block of 32 rows, no slab is named by more than 2 rows.
All inputs are finite; a program needn't handle non-finite values. No bound on the sum of `wall_mask` on one device may be relied on, other than what follows from the above.
Results may differ from the reference program's by a relative error of at most 0.0003.
Values may be sent and summed in bfloat16 or wider, within the bound.
A program may use at most 32 MiB of HBM per device.

```python
import math
import jax
import jax.numpy as jnp
import numpy as np
from jax import lax

CX = 4
NY = 512
NZ = 128
R_DEV = 32
NRATES = 8
NX = 192
NCOND = 16
NTGT = 1536
CAP = 2
N_SLAB = 48


def with_ends(entries, own_key, smallest, high):
    place = [jax.random.randint(jax.random.fold_in(own_key, axis), (), 0, length) for axis, length in enumerate(entries.shape)]
    longest = entries.shape.index(max(entries.shape))
    next_to = place[:longest] + [(place[longest] + 1) % entries.shape[longest]] + place[longest + 1:]
    return entries.at[tuple(place)].set(smallest).at[tuple(next_to)].set(high)


def block_levels(rng, extent, shards, least, largest):
    factor_of = 1.0
    for position, parts in shards:
        heights = jax.random.uniform(jax.random.fold_in(jax.random.fold_in(rng, 6), position), (parts,), jnp.float32, least / len(shards), largest / len(shards))
        factor_of = factor_of * jnp.repeat(jnp.exp(heights), extent[position] // parts).reshape((-1,) + (1,) * (len(extent) - 1 - position))
    return factor_of


def routed_block(key, own, number, rows, number_of, top, bound, slope):
    order = jax.random.permutation(key, number_of)
    crowded, ordinary = shares(number_of, rows * top, bound, slope, True), shares(number_of, rows * top, bound, slope, False)
    places = jnp.arange(number_of)

    def named(tallies, rotation):
        used = int((tallies > 0).sum())
        fixed = max(1, used // 4)
        passed = fixed + (places - fixed + rotation * (used - fixed)) % max(1, number_of - fixed)
        return jnp.zeros((number_of,), jnp.int32).at[order[jnp.where(places < fixed, places, passed)]].set(jnp.asarray(tallies, jnp.int32))

    tallies = jnp.where(number % 4 == 0, named(crowded, number // 4), named(ordinary, number - number // 4 - 1))
    mixed = jax.random.permutation(jax.random.fold_in(own, 3), number_of)
    donor, receiver = mixed[0:number_of // 2 * 2:2], mixed[1:number_of // 2 * 2:2]
    margin = jnp.minimum(tallies[donor] - 1, bound - tallies[receiver]) // 2
    margin = jnp.where((donor == order[0]) | (receiver == order[0]) | (tallies[receiver] == 0), 0, jnp.maximum(margin, 0))
    passed = jax.random.randint(jax.random.fold_in(own, 4), (number_of // 2,), 0, 1 << 20) % (margin + 1)
    tallies = tallies.at[donor].add(-passed).at[receiver].add(passed)
    items = jnp.searchsorted(jnp.cumsum(tallies), jnp.arange(rows * top), side="right").astype(jnp.int32)
    listing = items.reshape(top, rows).T
    listing = listing[jax.random.permutation(jax.random.fold_in(own, 1), rows)]
    rotation = jax.random.randint(jax.random.fold_in(own, 2), (rows, 1), 0, top)
    return jnp.take_along_axis(listing, (jnp.arange(top)[None, :] + rotation) % top, axis=1)


def shares(amount, total, limit, lean, full):
    portions = [(1 << 20) // math.isqrt(grade ** lean) + 1 for grade in range(1, amount + 1)]
    largest = limit if full else min(limit, max(-(-total // amount), total * portions[0] // sum(portions)))
    least = 1 if total - largest >= amount - 1 else 0
    holding, rest = [largest] + [least] * (amount - 1), total - largest - least * (amount - 1)
    while rest > 0:
        candidates = [i for i in range(1, amount) if holding[i] < largest] or [i for i in range(1, amount) if holding[i] < limit]
        mass, remaining = sum([portions[i] for i in candidates]), rest
        for i in candidates:
            extra = min(limit - holding[i], max(1, remaining * portions[i] // mass), rest)
            holding[i] = holding[i] + extra
            rest = rest - extra
    return np.array(holding)


def bell_draw(rng, dims, spread, most, split=(), dtype=jnp.bfloat16):
    drawn = jax.random.normal(rng, dims, jnp.float32) * spread
    if len(split) > 0:
        drawn = block_levels(rng, dims, split, -0.22, 0.18) * drawn
    return jnp.clip(drawn, min=-most, max=most).astype(dtype)


def setup_inputs(seed: int = 0) -> dict:
    arg_keys = jax.random.split(jax.random.key(seed), 9)
    adjoint = bell_draw(arg_keys[0], (NCOND, NX, NY, NZ), 1.0, 6.0, ((0, 16), (1, 48)), jnp.float32)
    phase = jnp.clip(jax.random.uniform(arg_keys[1], (NCOND, NX, NY, NZ), jnp.float32, -1.09375, 1.09375) * block_levels(arg_keys[1], (NCOND, NX, NY, NZ), ((0, 16), (1, 48)), -0.4, 0.0), -1.09375, 1.09375).astype(jnp.bfloat16)
    targets = jnp.clip(jax.random.uniform(arg_keys[2], (NCOND, NTGT, NZ), jnp.float32, -1.0, 1.0) * block_levels(arg_keys[2], (NCOND, NTGT, NZ), ((0, 16), (1, 48)), -0.4, 0.0), -1.0, 1.0).astype(jnp.bfloat16)
    owners_keys = jax.random.split(jax.random.fold_in(arg_keys[3], 1), NCOND * NTGT // R_DEV)
    owners_turns = jax.random.permutation(jax.random.fold_in(arg_keys[3], 3), NCOND * NTGT // R_DEV)
    owners = jax.vmap(lambda own, number: routed_block(jax.random.fold_in(arg_keys[3], 2), own, number, R_DEV, N_SLAB, 1, CAP, 2))(owners_keys, owners_turns).reshape((NCOND, NTGT, 1))
    target_cell = with_ends(jax.random.randint(arg_keys[4], (NCOND, NTGT), 0, CX * NY), jax.random.fold_in(arg_keys[4], 1), 0, (CX * NY) - 1).astype(jnp.int32)
    rate_index = with_ends(jax.random.randint(arg_keys[5], (NCOND,), 0, NRATES), jax.random.fold_in(arg_keys[5], 1), 0, NRATES - 1).astype(jnp.int32)
    inflow_rates = jnp.clip(jnp.exp(jax.random.uniform(arg_keys[6], (NRATES,), jnp.float32, math.log(0.5), math.log(2.0))), 0.5, 2.0)
    wall_mask = with_ends((jax.random.randint(arg_keys[7], (2, NX, NY), 0, 2) < 1).astype(jnp.int32), jax.random.fold_in(arg_keys[7], 1), 0, 1)
    return dict(adjoint=adjoint, phase=phase, targets=targets, owners=owners, target_cell=target_cell, rate_index=rate_index, inflow_rates=inflow_rates, wall_mask=wall_mask)


mobility_step = 0.02
stiffness_step = 0.01
transport_step = 0.125
wall_weight = 0.25


def inner_laplacian(field):
    center = field[1:-1]
    along_y = jnp.pad(center, ((0, 0), (1, 1), (0, 0)))
    along_z = jnp.pad(center, ((0, 0), (0, 0), (1, 1)))
    return (field[2:] + field[:-2] + along_y[:, 2:] + along_y[:, :-2]
            + along_z[:, :, 2:] + along_z[:, :, :-2] - 6.0 * center)


def within_grid(length, first_row, grid_rows):
    placed = first_row + jnp.arange(length)
    within = (placed >= 0) & (placed < grid_rows)
    return within.astype(jnp.float32)[:, None, None]


def adjoint_step(extended, curvature, inflow, first_row, grid_rows):
    length = extended.shape[0]
    first_lap = inner_laplacian(extended) * within_grid(length - 2, first_row + 1, grid_rows)
    second_lap = inner_laplacian(first_lap)
    center = extended[2:-2]
    column_depth = extended.shape[2]
    height = (jnp.arange(column_depth).astype(jnp.float32) + 0.5) / column_depth
    profile = 4.0 * height * (1.0 - height)
    padded = jnp.pad(center, ((0, 0), (1, 1), (0, 0)))
    transport = (padded[:, 2:] - padded[:, :-2]) * profile
    updated = (center + mobility_step * curvature * first_lap[1:-1]
               - stiffness_step * second_lap + transport_step * inflow * transport)
    return updated * within_grid(length - 4, first_row + 2, grid_rows)


def wall_term(state, phase32, wall_mask):
    lower_wall = (1.0 - phase32[:, :, 0] ** 2) * state[:, :, 0]
    upper_wall = (1.0 - phase32[:, :, -1] ** 2) * state[:, :, -1]
    return wall_weight * wall_mask.astype(jnp.float32) * jnp.stack([lower_wall, upper_wall])


def one_condition(adjoint_now, phase_now, target_rows, owner_rows, cell_rows, inflow, wall_mask):
    phase32 = phase_now.astype(jnp.float32)
    curvature = 3.0 * phase32 * phase32 - 1.0
    grid_rows = adjoint_now.shape[0]
    state = adjoint_now
    gradient = jnp.zeros(wall_mask.shape, jnp.float32)
    for sweep in range(2):
        extended = jnp.pad(state, ((2, 2), (0, 0), (0, 0)))
        state = adjoint_step(extended, curvature, inflow, -2, grid_rows)
        gradient = gradient + wall_term(state, phase32, wall_mask)
    row_index = (owner_rows[:, 0].astype(jnp.int32) * (CX * NY) + cell_rows.astype(jnp.int32)).astype(jnp.int32)
    flat_phase = phase32.reshape(-1, NZ)
    source = flat_phase[row_index] - target_rows.astype(jnp.float32)
    state = state.reshape(-1, NZ).at[row_index].add(source).reshape(state.shape)
    return state, gradient


def reference(adjoint, phase, targets, owners, target_cell, rate_index, inflow_rates, wall_mask):
    def per_condition(running, members):
        adjoint_now, phase_now, target_rows, owner_rows, cell_rows, chosen = members
        inflow = inflow_rates[chosen]
        state, gradient = one_condition(adjoint_now, phase_now, target_rows, owner_rows, cell_rows, inflow, wall_mask)
        return running + gradient, state
    initial = jnp.zeros(wall_mask.shape, jnp.float32)
    gradient, states = lax.scan(per_condition, initial, (adjoint, phase, targets, owners, target_cell, rate_index))
    return states, gradient
```

```python
import functools

import jax
import jax.numpy as jnp
from jax import lax
from jax.experimental import pallas as pl
from jax.experimental.pallas import tpu as pltpu
from jax.sharding import PartitionSpec as P

MESH = pl.DeviceIdType.MESH
F32 = jnp.float32
BF16 = jnp.bfloat16

mobility_step = 0.02
stiffness_step = 0.01
transport_step = 0.125
wall_weight = 0.25

CHUNKS = 4
PAD = 8


def kernel(
    n_cond, n_slab, adj, ph, tgt, own, cell, ridx, rates, mask, out, grad,
    S, PB, F, S1, OB, H, LO, SB, RB, tv, ov, cv, mv, ST, RT, TA, G, GS, RR, FIN, tot,
    in_sem, ss, rs, ts, tr, gs, gr, fs, fr, out_sem, go, go2,
):
    ny = S.shape[1] - 2 * PAD
    nz = S.shape[2]
    nx = S.shape[0]
    c = lax.axis_index("cond")
    me = lax.axis_index("slab")
    last = n_slab - 1
    has = (me > 0, me < last)
    peer = (me - 1, me + 1)
    near = (0, nx - 1)
    far = (1, nx - 2)
    step = ny // CHUNKS

    loads = [pltpu.make_async_copy(adj.at[0, j], S.at[j, pl.ds(PAD, ny)], in_sem.at[j]) for j in range(nx)]
    ph_load = pltpu.make_async_copy(ph.at[0], PB, in_sem.at[nx])
    small = [
        pltpu.make_async_copy(tgt.at[0], tv, in_sem.at[nx + 1]),
        pltpu.make_async_copy(own, ov, in_sem.at[nx + 2]),
        pltpu.make_async_copy(cell, cv, in_sem.at[nx + 3]),
        pltpu.make_async_copy(mask, mv, in_sem.at[nx + 4]),
    ]
    for j in (0, nx - 1, 1, nx - 2):
        loads[j].start()
    for cp in small:
        cp.start()
    ph_load.start()

    bar = pltpu.get_barrier_semaphore()
    for s in range(2):
        @pl.when(has[s])
        def _():
            pl.semaphore_signal(bar, inc=1, device_id=(c, peer[s]), device_id_type=MESH)

    @pl.when(me < last - 1)
    def _():
        pl.semaphore_signal(bar, inc=1, device_id=(c, last), device_id_type=MESH)

    @pl.when(c > 0)
    def _():
        pl.semaphore_signal(bar, inc=1, device_id=(0, me), device_id_type=MESH)

    lane = lax.broadcasted_iota(jnp.int32, (1, nz), 1)
    keep_lo = (lane > 0).astype(F32)
    keep_hi = (lane < nz - 1).astype(F32)
    height = (lane.astype(F32) + 0.5) / nz
    profile = 4.0 * height * (1.0 - height)
    inflow = F32(0.0)
    for i in range(rates.shape[0]):
        inflow = inflow + jnp.where(ridx[0] == i, rates[i], 0.0)
    drift = (transport_step * inflow) * profile

    def in_plane(ref, j, r, n):
        x = ref[j, pl.ds(r + PAD, n), :]
        zsum = pltpu.roll(x, 1, 1) * keep_lo + pltpu.roll(x, nz - 1, 1) * keep_hi
        return zsum + ref[j, pl.ds(r + (PAD - 1), n), :] + ref[j, pl.ds(r + (PAD + 1), n), :] - 6.0 * x

    def rows(lo, hi, n, body):
        def run(i, _):
            body(pl.multiple_of(lo + i * n, 16))
            return 0
        lax.fori_loop(0, (hi - lo) // n, run, 0)

    def mobility(j, r, n):
        p = PB[j, pl.ds(r, n), :].astype(F32)
        return (3.0 * mobility_step) * (p * p) - mobility_step

    zpad = jnp.zeros((PAD, nz), F32)
    for ref in (S, F, S1):
        for j in range(nx):
            ref[j, pl.ds(0, PAD), :] = zpad
            ref[j, pl.ds(PAD + ny, PAD), :] = zpad
    for ref in (H, LO):
        for j in range(2):
            ref[j, pl.ds(0, PAD), :] = zpad
            ref[j, pl.ds(PAD + ny, PAD), :] = zpad

    def split(ref, phase, s, lo, hi):
        def body(r):
            x = ref[near[s], pl.ds(r + PAD, 16), :]
            h = x.astype(BF16)
            SB[phase, s, 0, pl.ds(r, 16), :] = h
            LO[s, pl.ds(r + PAD, 16), :] = x - h.astype(F32)
        rows(lo, hi, 16, body)

    def residue(ref, phase, s, lo, hi):
        def body(r):
            q = -2.0 * stiffness_step * in_plane(LO, s, r, 16) - stiffness_step * ref[far[s], pl.ds(r + PAD, 16), :]
            SB[phase, s, 1, pl.ds(r, 16), :] = q.astype(BF16)
        rows(lo, hi, 16, body)

    def piece(phase, s, k, lo, hi, p):
        return pltpu.make_async_remote_copy(
            src_ref=SB.at[phase, s, p, pl.ds(lo, hi - lo)],
            dst_ref=RB.at[phase, 1 - s, p, pl.ds(lo, hi - lo)],
            send_sem=ss.at[phase, s, p, k],
            recv_sem=rs.at[phase, 1 - s, p, k],
            device_id=(c, peer[s]),
            device_id_type=MESH,
        )

    def landing(phase, s, k, lo, hi, p):
        return pltpu.make_async_remote_copy(
            src_ref=SB.at[phase, 1 - s, p, pl.ds(lo, hi - lo)],
            dst_ref=RB.at[phase, s, p, pl.ds(lo, hi - lo)],
            send_sem=ss.at[phase, 1 - s, p, k],
            recv_sem=rs.at[phase, s, p, k],
            device_id=(c, peer[s]),
            device_id_type=MESH,
        )

    cuts = [[(k * step, (k + 1) * step) for k in range(CHUNKS)]]
    for lag in (32,):
        edges = [0] + [k * step - lag for k in range(1, CHUNKS)] + [ny]
        cuts.append(list(zip(edges[:-1], edges[1:])))

    def lagged(phase, k, lag):
        lo = 0 if k == 0 else cuts[phase][k][0] - lag
        hi = ny if k == CHUNKS - 1 else cuts[phase][k][1] - lag
        return lo, hi

    for s in range(2):
        loads[near[s]].wait()
        split(S, 0, s, 0, ny)
        loads[far[s]].wait()
        residue(S, 0, s, 0, ny)

    greeted = has[0].astype(jnp.int32) + has[1].astype(jnp.int32)
    greeted = greeted + jnp.where(me == last, last - 1, 0) + jnp.where(c == 0, n_cond - 1, 0)
    pl.semaphore_wait(bar, greeted)
    for k in range(CHUNKS):
        for s in range(2):
            @pl.when(has[s])
            def _():
                for p in range(2):
                    piece(0, s, k, *cuts[0][k], p).start()

    @pl.when(me == last)
    def _():
        def tell(d, _):
            pl.semaphore_signal(go, inc=1, device_id=(c, d), device_id_type=MESH)
            return 0
        lax.fori_loop(0, last, tell, 0)

    @pl.when(c == 0)
    def _():
        def tell(d, _):
            pl.semaphore_signal(go2, inc=1, device_id=(d, me), device_id_type=MESH)
            return 0
        lax.fori_loop(1, n_cond, tell, 0)

    for cp in small:
        cp.wait()
    n_rows = tv.shape[0]
    match = (ov[...] == lax.broadcasted_iota(jnp.int32, (n_slab, n_rows), 0)).astype(F32)
    upper = (
        lax.broadcasted_iota(jnp.int32, (n_rows, n_rows), 0) < lax.broadcasted_iota(jnp.int32, (n_rows, n_rows), 1)
    ).astype(BF16)
    earlier = jnp.dot(match.astype(BF16), upper, preferred_element_type=F32)
    first = jnp.where(earlier < 0.5, match, 0.0)
    second = match - first
    code = cv[...].astype(F32) + 16.0
    lanes = lax.broadcasted_iota(jnp.int32, (n_slab, nz), 1)
    high = jnp.zeros((n_slab, nz), F32)
    low = jnp.zeros((n_slab, nz), F32)
    for i, pick in enumerate((first, second)):
        ST[:, i, :] = jnp.dot(pick.astype(BF16), tv[...], preferred_element_type=F32).astype(ST.dtype)
        mine = jnp.sum(pick * code, axis=1, keepdims=True)
        hi_part = jnp.floor(mine * (1.0 / 16.0))
        here = lanes == me + i * n_slab
        high = jnp.where(here, hi_part, high)
        low = jnp.where(here, mine - 16.0 * hi_part, low)
    ST[:, 2, :] = high.astype(ST.dtype)
    ST[:, 3, :] = low.astype(ST.dtype)
    RT[me] = ST[me]

    def row_copy(d, slot):
        return pltpu.make_async_remote_copy(
            src_ref=ST.at[d], dst_ref=RT.at[slot], send_sem=ts.at[d], recv_sem=tr.at[slot],
            device_id=(c, d), device_id_type=MESH,
        )

    def send_rows():
        @pl.when(me < last)
        def _():
            pl.semaphore_wait(go, 1)

        def one(i, _):
            row_copy(lax.rem(me + i, n_slab), me).start()
            return 0
        lax.fori_loop(1, n_slab, one, 0)

    late = me >= n_slab - n_slab // 6
    middle = jnp.logical_and(me >= n_slab // 2, jnp.logical_not(late))

    @pl.when(late)
    def _():
        send_rows()

    ghost = (has[0].astype(F32), has[1].astype(F32))

    def local_step(src, dst, padded):
        def laps(r):
            for j in range(nx):
                v = in_plane(src, j, r, 16)
                for o in (j - 1, j + 1):
                    if 0 <= o < nx:
                        v = v + src[o, pl.ds(r + PAD, 16), :]
                F[j, pl.ds(r + PAD, 16), :] = v
        rows(0, ny, 16, laps)

        def update(r):
            for j in range(nx):
                lap2 = in_plane(F, j, r, 16)
                for o in (j - 1, j + 1):
                    if 0 <= o < nx:
                        lap2 = lap2 + F[o, pl.ds(r + PAD, 16), :]
                x = src[j, pl.ds(r + PAD, 16), :]
                for s in range(2):
                    if j == near[s]:
                        lap2 = lap2 + ghost[s] * x
                moved = src[j, pl.ds(r + (PAD + 1), 16), :] - src[j, pl.ds(r + (PAD - 1), 16), :]
                v = x + mobility(j, r, 16) * F[j, pl.ds(r + PAD, 16), :] - stiffness_step * lap2 + drift * moved
                dst[j, pl.ds(r + padded, 16), :] = v
        rows(0, ny, 16, update)

    def unpack(phase, s, lo, hi):
        def body(r):
            H[s, pl.ds(r + PAD, 16), :] = RB[phase, s, 0, pl.ds(r, 16), :].astype(F32)
        rows(lo, hi, 16, body)

    def correct(phase, dst, padded, s, lo, hi):
        def body(r):
            h = H[s, pl.ds(r + PAD, 16), :]
            v = dst[near[s], pl.ds(r + padded, 16), :] + mobility(near[s], r, 16) * h
            v = v - 2.0 * stiffness_step * in_plane(H, s, r, 16) + RB[phase, s, 1, pl.ds(r, 16), :].astype(F32)
            dst[near[s], pl.ds(r + padded, 16), :] = v
            dst[far[s], pl.ds(r + padded, 16), :] = dst[far[s], pl.ds(r + padded, 16), :] - stiffness_step * h
        rows(lo, hi, 16, body)

    ph_load.wait()
    local_step(S, S1, PAD)
    for k in range(CHUNKS):
        for s in range(2):
            @pl.when(has[s])
            def _():
                for p in range(2):
                    landing(0, s, k, *cuts[0][k], p).wait_recv()
                unpack(0, s, *cuts[0][k])
                lo, hi = lagged(0, k, 16)
                correct(0, S1, PAD, s, lo, hi)
                split(S1, 1, s, lo, hi)
                residue(S1, 1, s, *cuts[1][k])
                for p in range(2):
                    piece(1, s, k, *cuts[1][k], p).start()
        if k == 1:
            @pl.when(middle)
            def _():
                send_rows()

    @pl.when(me < n_slab // 2)
    def _():
        send_rows()

    local_step(S1, OB, 0)

    def walls(lo, hi):
        for b in range(lo // nz, hi // nz):
            total = jnp.zeros((2 * nx, nz), F32)
            for j in range(nx):
                p = PB[j, pl.ds(b * nz, nz), :].astype(F32)
                x = (1.0 - p * p) * (S1[j, pl.ds(b * nz + PAD, nz), :] + OB[j, pl.ds(b * nz, nz), :])
                row = lax.broadcasted_iota(jnp.int32, (2 * nx, nz), 0)
                col = lax.broadcasted_iota(jnp.int32, (2 * nx, nz), 1)
                pick = jnp.logical_or(
                    jnp.logical_and(row == j, col == 0), jnp.logical_and(row == nx + j, col == nz - 1)
                ).astype(F32)
                total = total + lax.dot_general(
                    pick, x, (((1,), (1,)), ((), ())), precision=lax.Precision.HIGHEST, preferred_element_type=F32
                )
            G[:, pl.ds(b * nz, nz)] = total

    done = 0
    for k in range(CHUNKS):
        lo, hi = lagged(1, k, 16)
        for s in range(2):
            @pl.when(has[s])
            def _():
                for p in range(2):
                    landing(1, s, k, *cuts[1][k], p).wait_recv()
                unpack(1, s, *cuts[1][k])
                correct(1, OB, 0, s, lo, hi)
        ready = hi // nz * nz
        walls(done, ready)
        done = ready

    n_red = GS.shape[0]
    stride = n_cond // n_red
    for r in range(n_red):
        GS[r] = G[r : r + 1, :]

    @pl.when(c > 0)
    def _():
        pl.semaphore_wait(go2, 1)

    def part(r, slot):
        return pltpu.make_async_remote_copy(
            src_ref=GS.at[r], dst_ref=RR.at[slot], send_sem=gs.at[r], recv_sem=gr.at[slot],
            device_id=(r * stride, me), device_id_type=MESH,
        )

    def whole(d, r):
        return pltpu.make_async_remote_copy(
            src_ref=tot, dst_ref=FIN.at[r], send_sem=fs.at[d], recv_sem=fr.at[r],
            device_id=(d, me), device_id_type=MESH,
        )

    for r in range(n_red):
        @pl.when(c != r * stride)
        def _():
            part(r, c).start()

    mine_r = c // stride
    reducer = lax.rem(c, stride) == 0

    def rows_in(i, _):
        d = lax.rem(me + i, n_slab)
        row_copy(d, d).wait_recv()
        return 0
    lax.fori_loop(1, n_slab, rows_in, 0)
    TA[...] = jnp.zeros_like(TA)
    for i in range(2):
        TA[pl.ds(i * n_slab, n_slab), pl.ds(0, nz)] = RT[:, i, :].astype(BF16)
    TA[:, pl.ds(nz, nz)] = jnp.ones((nz, nz), BF16)
    hi_sum = jnp.sum(RT[:, 2, :].astype(F32), axis=0, keepdims=True)
    lo_sum = jnp.sum(RT[:, 3, :].astype(F32), axis=0, keepdims=True)
    where_to = ((hi_sum - 1.0) * 16.0 + lo_sum).astype(jnp.int32)
    per = ny // nz
    for j in range(nx):
        def inject(b, _):
            r = pl.multiple_of(b * nz, nz)
            at = lax.broadcasted_iota(jnp.int32, (nz, nz), 0) + (j * ny + r)
            hit = (at == where_to).astype(F32).astype(BF16)
            both = jnp.dot(hit, TA[...], preferred_element_type=F32)
            p = PB[j, pl.ds(r, nz), :].astype(F32)
            OB[j, pl.ds(r, nz), :] = OB[j, pl.ds(r, nz), :] + (p * both[:, nz:] - both[:, :nz])
            return 0
        lax.fori_loop(0, per, inject, 0)
        pltpu.make_async_copy(OB.at[j], out.at[0, j], out_sem.at[j]).start()

    @pl.when(reducer)
    def _():
        tot[...] = GS[mine_r]

        def add(i, _):
            d = lax.rem(c + i, n_cond)
            part(mine_r, d).wait_recv()
            tot[...] = tot[...] + RR[d]
            return 0
        lax.fori_loop(1, n_cond, add, 0)

        def tell(i, _):
            whole(lax.rem(c + i, n_cond), mine_r).start()
            return 0
        lax.fori_loop(1, n_cond, tell, 0)
        FIN[mine_r] = tot[...]

    for r in range(n_red):
        @pl.when(c != r * stride)
        def _():
            whole(c, r).wait_recv()
    for w in range(2):
        for x in range(nx):
            grad[w, x : x + 1, :] = (wall_weight * mv[w, x : x + 1, :].astype(F32)) * FIN[w * nx + x]

    for phase in range(2):
        for s in range(2):
            @pl.when(has[s])
            def _():
                for k in range(CHUNKS):
                    for p in range(2):
                        piece(phase, s, k, *cuts[phase][k], p).wait_send()

    def rows_out(i, _):
        d = lax.rem(me + i, n_slab)
        row_copy(d, me).wait_send()
        return 0
    lax.fori_loop(1, n_slab, rows_out, 0)
    for r in range(n_red):
        @pl.when(c != r * stride)
        def _():
            part(r, c).wait_send()

    @pl.when(reducer)
    def _():
        def sent(i, _):
            whole(lax.rem(c + i, n_cond), mine_r).wait_send()
            return 0
        lax.fori_loop(1, n_cond, sent, 0)
    for j in range(nx):
        pltpu.make_async_copy(OB.at[j], out.at[0, j], out_sem.at[j]).wait()


def on_device(adjoint, phase, targets, owners, target_cell, rate_index, inflow_rates, wall_mask):
    n_cond = lax.axis_size("cond")
    n_slab = lax.axis_size("slab")
    _, nx, ny, nz = adjoint.shape
    n_rows = targets.shape[1]
    n_red = 2 * nx
    any_space = pl.BlockSpec(memory_space=pl.ANY)
    smem = pl.BlockSpec(memory_space=pltpu.SMEM)
    dma = pltpu.SemaphoreType.DMA
    padded = ny + 2 * PAD
    call = pl.pallas_call(
        functools.partial(kernel, n_cond, n_slab),
        out_shape=(
            jax.ShapeDtypeStruct(adjoint.shape, F32),
            jax.ShapeDtypeStruct(wall_mask.shape, F32),
        ),
        in_specs=[any_space] * 5 + [smem, smem, any_space],
        out_specs=(any_space, pl.BlockSpec(memory_space=pltpu.VMEM)),
        scratch_shapes=[
            pltpu.VMEM((nx, padded, nz), F32),
            pltpu.VMEM((nx, ny, nz), BF16),
            pltpu.VMEM((nx, padded, nz), F32),
            pltpu.VMEM((nx, padded, nz), F32),
            pltpu.VMEM((nx, ny, nz), F32),
            pltpu.VMEM((2, padded, nz), F32),
            pltpu.VMEM((2, padded, nz), F32),
            pltpu.VMEM((2, 2, 2, ny, nz), BF16),
            pltpu.VMEM((2, 2, 2, ny, nz), BF16),
            pltpu.VMEM((n_rows, nz), BF16),
            pltpu.VMEM((1, n_rows), jnp.int32),
            pltpu.VMEM((1, n_rows), jnp.int32),
            pltpu.VMEM(wall_mask.shape, jnp.int32),
            pltpu.VMEM((n_slab, 4, nz), ROW),
            pltpu.VMEM((n_slab, 4, nz), ROW),
            pltpu.VMEM((nz, 2 * nz), BF16),
            pltpu.VMEM((n_red, ny), F32),
            pltpu.VMEM((n_red, 1, ny), F32),
            pltpu.VMEM((n_cond, 1, ny), F32),
            pltpu.VMEM((n_red, 1, ny), F32),
            pltpu.VMEM((1, ny), F32),
            dma((nx + 5,)),
            dma((2, 2, 2, CHUNKS)),
            dma((2, 2, 2, CHUNKS)),
            dma((n_slab,)),
            dma((n_slab,)),
            dma((n_red,)),
            dma((n_cond,)),
            dma((n_cond,)),
            dma((n_red,)),
            dma((nx,)),
            pltpu.SemaphoreType.REGULAR,
            pltpu.SemaphoreType.REGULAR,
        ],
        compiler_params=pltpu.CompilerParams(
            collective_id=0, has_side_effects=True, vmem_limit_bytes=40 * 1024 * 1024
        ),
    )
    owner_row = owners.reshape(1, n_rows)
    return call(adjoint, phase, targets, owner_row, target_cell, rate_index, inflow_rates, wall_mask)


ROW = F32


def solution(mesh):
    in_specs = (
        P("cond", "slab", None, None),
        P("cond", "slab", None, None),
        P("cond", "slab", None),
        P("cond", "slab", None),
        P("cond", "slab"),
        P("cond"),
        P(),
        P(None, "slab", None),
    )
    out_specs = (P("cond", "slab", None, None), P(None, "slab", None))
    return jax.shard_map(
        on_device, mesh=mesh, in_specs=in_specs, out_specs=out_specs, check_vma=False
    )
```

```python
import functools

import jax
import jax.numpy as jnp
from jax import lax
from jax.experimental import pallas as pl
from jax.experimental.pallas import tpu as pltpu
from jax.sharding import PartitionSpec as P

MESH = pl.DeviceIdType.MESH
F32 = jnp.float32
BF16 = jnp.bfloat16

mobility_step = 0.02
stiffness_step = 0.01
transport_step = 0.125
wall_weight = 0.25

CHUNKS = 4
HELD = 2
PAD = 8


def kernel(
    n_cond, n_slab, adj, ph, tgt, own, cell, ridx, rates, mask, out, grad,
    S, PB, F, S1, H, LO, SB, RB, tv, ov, cv, mv, fv, ST, RT, TA, BW, EP, WS, WR, GS, RR, FIN, tot,
    in_sem, ss, rs, ts, tr, gs, gr, fs, fr, ws, wr, go, go2, up,
):
    OB = out.at[0]
    ny = S.shape[1] - 2 * PAD
    nz = S.shape[2]
    nx = S.shape[0]
    c = lax.axis_index("cond")
    me = lax.axis_index("slab")
    last = n_slab - 1
    has = (me > 0, me < last)
    peer = (me - 1, me + 1)
    near = (0, nx - 1)
    far = (1, nx - 2)
    step = ny // CHUNKS

    loads = [pltpu.make_async_copy(adj.at[0, j], S.at[j, pl.ds(PAD, ny)], in_sem.at[j]) for j in range(nx)]
    ph_load = pltpu.make_async_copy(ph.at[0], PB, in_sem.at[nx])
    small = [
        pltpu.make_async_copy(tgt.at[0], tv, in_sem.at[nx + 1]),
        pltpu.make_async_copy(own, ov, in_sem.at[nx + 2]),
        pltpu.make_async_copy(cell, cv, in_sem.at[nx + 3]),
        pltpu.make_async_copy(mask, mv, in_sem.at[nx + 4]),
        pltpu.make_async_copy(rates, fv, in_sem.at[nx + 5]),
    ]
    for j in (0, nx - 1, 1, nx - 2):
        loads[j].start()
    for cp in small:
        cp.start()
    ph_load.start()

    bar = pltpu.get_barrier_semaphore()
    for s in range(2):
        @pl.when(has[s])
        def _():
            pl.semaphore_signal(bar, inc=1, device_id=(c, peer[s]), device_id_type=MESH)

    half = n_slab // 2
    upper = me >= half
    hub = jnp.where(upper, last, half - 1)

    @pl.when(me < hub - 1)
    def _():
        pl.semaphore_signal(bar, inc=1, device_id=(c, hub), device_id_type=MESH)

    @pl.when(c > 0)
    def _():
        pl.semaphore_signal(bar, inc=1, device_id=(0, me), device_id_type=MESH)

    @pl.when(jnp.logical_not(upper))
    def _():
        def greet(d, _):
            pl.semaphore_signal(bar, inc=1, device_id=(c, d), device_id_type=MESH)
            return 0
        lax.fori_loop(jnp.where(me == half - 1, half + 1, half), n_slab, greet, 0)

    lane = lax.broadcasted_iota(jnp.int32, (1, nz), 1)
    keep_lo = (lane > 0).astype(F32)
    keep_hi = (lane < nz - 1).astype(F32)
    height = (lane.astype(F32) + 0.5) / nz
    profile = 4.0 * height * (1.0 - height)

    def in_plane(ref, j, r, n):
        x = ref[j, pl.ds(r + PAD, n), :]
        zsum = pltpu.roll(x, 1, 1) * keep_lo + pltpu.roll(x, nz - 1, 1) * keep_hi
        return zsum + ref[j, pl.ds(r + (PAD - 1), n), :] + ref[j, pl.ds(r + (PAD + 1), n), :] - 6.0 * x

    def rows(lo, hi, body):
        r = lo
        while r < hi:
            n = min(64, hi - r)
            body(r, n)
            r += n

    def mobility(j, r, n):
        p = PB[j, pl.ds(r, n), :].astype(F32)
        return (3.0 * mobility_step) * (p * p) - mobility_step

    zpad = jnp.zeros((PAD, nz), F32)
    for ref in (S, F, S1):
        for j in range(nx):
            ref[j, pl.ds(0, PAD), :] = zpad
            ref[j, pl.ds(PAD + ny, PAD), :] = zpad
    for ref in (H, LO):
        for j in range(2):
            ref[j, pl.ds(0, PAD), :] = zpad
            ref[j, pl.ds(PAD + ny, PAD), :] = zpad

    def split(ref, phase, s, lo, hi):
        def body(r, n):
            x = ref[near[s], pl.ds(r + PAD, n), :]
            h = x.astype(BF16)
            SB[phase, s, 0, pl.ds(r, n), :] = h
            LO[s, pl.ds(r + PAD, n), :] = x - h.astype(F32)
        rows(lo, hi, body)

    def residue(ref, phase, s, lo, hi):
        def body(r, n):
            q = -2.0 * stiffness_step * in_plane(LO, s, r, n) - stiffness_step * ref[far[s], pl.ds(r + PAD, n), :]
            SB[phase, s, 1, pl.ds(r, n), :] = q.astype(BF16)
        rows(lo, hi, body)

    def piece(phase, s, k, lo, hi):
        return pltpu.make_async_remote_copy(
            src_ref=SB.at[phase, s, :, pl.ds(lo, hi - lo)],
            dst_ref=RB.at[phase, 1 - s, :, pl.ds(lo, hi - lo)],
            send_sem=ss.at[phase, s, k],
            recv_sem=rs.at[phase, 1 - s, k],
            device_id=(c, peer[s]),
            device_id_type=MESH,
        )

    def landing(phase, s, k, lo, hi):
        return pltpu.make_async_remote_copy(
            src_ref=SB.at[phase, 1 - s, :, pl.ds(lo, hi - lo)],
            dst_ref=RB.at[phase, s, :, pl.ds(lo, hi - lo)],
            send_sem=ss.at[phase, 1 - s, k],
            recv_sem=rs.at[phase, s, k],
            device_id=(c, peer[s]),
            device_id_type=MESH,
        )

    cuts = [[(k * step, (k + 1) * step) for k in range(CHUNKS)]]
    for lag in (32,):
        edges = [0] + [k * step - lag for k in range(1, CHUNKS)] + [ny]
        cuts.append(list(zip(edges[:-1], edges[1:])))

    def lagged(phase, k, lag):
        lo = 0 if k == 0 else cuts[phase][k][0] - lag
        hi = ny if k == CHUNKS - 1 else cuts[phase][k][1] - lag
        return lo, hi

    for s in range(2):
        loads[near[s]].wait()
        split(S, 0, s, 0, ny)
        loads[far[s]].wait()
        residue(S, 0, s, 0, ny)

    greeted = has[0].astype(jnp.int32) + has[1].astype(jnp.int32)
    greeted = greeted + jnp.where(me == hub, half - 2, 0) + jnp.where(c == 0, n_cond - 1, 0)
    greeted = greeted + jnp.where(upper, half, 0) - jnp.where(me == half, 1, 0)
    pl.semaphore_wait(bar, greeted)
    for s in range(2):
        @pl.when(has[s])
        def _():
            piece(0, s, 0, *cuts[0][0]).start()

    for cp in small:
        cp.wait()
    entry = lax.broadcasted_iota(jnp.int32, fv.shape, 1)
    inflow = jnp.sum(jnp.where(entry == ridx[0], fv[...], 0.0), axis=1, keepdims=True)
    drift = (transport_step * inflow) * profile
    n_rows = tv.shape[0]
    match = (ov[...] == lax.broadcasted_iota(jnp.int32, (n_slab, n_rows), 0)).astype(F32)
    prior = (
        lax.broadcasted_iota(jnp.int32, (n_rows, n_rows), 0) < lax.broadcasted_iota(jnp.int32, (n_rows, n_rows), 1)
    ).astype(BF16)
    earlier = jnp.dot(match.astype(BF16), prior, preferred_element_type=F32)
    first = jnp.where(earlier < 0.5, match, 0.0)
    second = match - first
    code = cv[...].astype(F32) + 16.0
    lanes = lax.broadcasted_iota(jnp.int32, (n_slab, nz), 1)
    high = jnp.zeros((n_slab, nz), F32)
    low = jnp.zeros((n_slab, nz), F32)
    for i, pick in enumerate((first, second)):
        ST[:, i, :] = jnp.dot(pick.astype(BF16), tv[...], preferred_element_type=F32).astype(ST.dtype)
        mine = jnp.sum(pick * code, axis=1, keepdims=True)
        hi_part = jnp.floor(mine * (1.0 / 16.0))
        here = lanes == me + i * n_slab
        high = jnp.where(here, hi_part, high)
        low = jnp.where(here, mine - 16.0 * hi_part, low)
    ST[:, 2, :] = high.astype(ST.dtype)
    ST[:, 3, :] = low.astype(ST.dtype)
    RT[me] = ST[me]

    def row_copy(d, slot):
        return pltpu.make_async_remote_copy(
            src_ref=ST.at[d], dst_ref=RT.at[slot], send_sem=ts.at[d], recv_sem=tr.at[slot],
            device_id=(c, d), device_id_type=MESH,
        )

    @pl.when(upper)
    def _():
        def one(d, _):
            row_copy(d, me).start()
            return 0
        lax.fori_loop(0, half, one, 0)
    for k in range(1, CHUNKS):
        for s in range(2):
            @pl.when(has[s])
            def _():
                piece(0, s, k, *cuts[0][k]).start()

    @pl.when(me == hub)
    def _():
        def tell(i, _):
            pl.semaphore_signal(go, inc=1, device_id=(c, me - i), device_id_type=MESH)
            return 0
        lax.fori_loop(1, half, tell, 0)

    @pl.when(upper)
    def _():
        def tell(d, _):
            pl.semaphore_signal(up, inc=1, device_id=(c, d), device_id_type=MESH)
            return 0
        lax.fori_loop(0, half, tell, 0)

    @pl.when(c == 0)
    def _():
        def tell(d, _):
            pl.semaphore_signal(go2, inc=1, device_id=(d, me), device_id_type=MESH)
            return 0
        lax.fori_loop(1, n_cond, tell, 0)

    first_own = jnp.where(upper, half, 0)

    def send_own_half():
        @pl.when(me != hub)
        def _():
            pl.semaphore_wait(go, 1)

        def one(i, _):
            row_copy(first_own + lax.rem(me - first_own + i, half), me).start()
            return 0
        lax.fori_loop(1, half, one, 0)

    def send_upper():
        pl.semaphore_wait(up, n_slab - half)

        def one(d, _):
            row_copy(d, me).start()
            return 0
        lax.fori_loop(half, n_slab, one, 0)

    ghost = (has[0].astype(F32), has[1].astype(F32))

    def local_step(src, dst, padded):
        def laps(r, n):
            for j in range(nx):
                v = in_plane(src, j, r, n)
                for o in (j - 1, j + 1):
                    if 0 <= o < nx:
                        v = v + src[o, pl.ds(r + PAD, n), :]
                F[j, pl.ds(r + PAD, n), :] = v
        rows(0, ny, laps)

        def update(r, n):
            for j in range(nx):
                lap2 = in_plane(F, j, r, n)
                for o in (j - 1, j + 1):
                    if 0 <= o < nx:
                        lap2 = lap2 + F[o, pl.ds(r + PAD, n), :]
                x = src[j, pl.ds(r + PAD, n), :]
                for s in range(2):
                    if j == near[s]:
                        lap2 = lap2 + ghost[s] * x
                moved = src[j, pl.ds(r + (PAD + 1), n), :] - src[j, pl.ds(r + (PAD - 1), n), :]
                v = x + mobility(j, r, n) * F[j, pl.ds(r + PAD, n), :] - stiffness_step * lap2 + drift * moved
                dst[j, pl.ds(r + padded, n), :] = v
        rows(0, ny, update)

    def unpack(phase, s, lo, hi):
        def body(r, n):
            H[s, pl.ds(r + PAD, n), :] = RB[phase, s, 0, pl.ds(r, n), :].astype(F32)
        rows(lo, hi, body)

    def correct(phase, dst, padded, s, lo, hi):
        def body(r, n):
            h = H[s, pl.ds(r + PAD, n), :]
            v = dst[near[s], pl.ds(r + padded, n), :] + mobility(near[s], r, n) * h
            v = v - 2.0 * stiffness_step * in_plane(H, s, r, n) + RB[phase, s, 1, pl.ds(r, n), :].astype(F32)
            dst[near[s], pl.ds(r + padded, n), :] = v
            dst[far[s], pl.ds(r + padded, n), :] = dst[far[s], pl.ds(r + padded, n), :] - stiffness_step * h
        rows(lo, hi, body)

    def chosen(places):
        row = lax.broadcasted_iota(jnp.int32, (8, nz), 0)
        col = lax.broadcasted_iota(jnp.int32, (8, nz), 1)
        pick = jnp.zeros((8, nz), F32)
        for i, z in places:
            pick = jnp.where(jnp.logical_and(row == i, col == z), 1.0, pick)
        return pick

    def turned(pick, x, **kw):
        return lax.dot_general(pick, x, (((1,), (1,)), ((), ())), preferred_element_type=F32, **kw)

    pick_wall = chosen(((0, 0), (1, nz - 1)))
    pick_t = chosen(((0, 0), (1, nz - 1), (2, 1), (3, nz - 2))).astype(BF16)
    pick_q = chosen(((4, 0), (5, nz - 1))).astype(BF16)

    def wall_lanes(s):
        WS[s] = (turned(pick_t, SB[1, s, 0]) + turned(pick_q, SB[1, s, 1])).astype(BF16)

    def wall_out(s):
        return pltpu.make_async_remote_copy(
            src_ref=WS.at[s], dst_ref=WR.at[1 - s], send_sem=ws.at[s], recv_sem=wr.at[1 - s],
            device_id=(c, peer[s]), device_id_type=MESH,
        )

    def wall_in(s):
        return pltpu.make_async_remote_copy(
            src_ref=WS.at[1 - s], dst_ref=WR.at[s], send_sem=ws.at[1 - s], recv_sem=wr.at[s],
            device_id=(c, peer[s]), device_id_type=MESH,
        )

    ph_load.wait()
    local_step(S, S1, PAD)
    for k in range(CHUNKS):
        for s in range(2):
            @pl.when(has[s])
            def _():
                landing(0, s, k, *cuts[0][k]).wait_recv()
                unpack(0, s, *cuts[0][k])
                lo, hi = lagged(0, k, 16)
                correct(0, S1, PAD, s, lo, hi)
                split(S1, 1, s, lo, hi)
                residue(S1, 1, s, *cuts[1][k])
                if k < HELD:
                    piece(1, s, k, *cuts[1][k]).start()
                if k == CHUNKS - 1:
                    wall_lanes(s)
                    wall_out(s).start()
        if k == 1:
            send_own_half()

    def release(k):
        for s in range(2):
            @pl.when(has[s])
            def _():
                piece(1, s, k, *cuts[1][k]).start()

    @pl.when(jnp.logical_not(upper))
    def _():
        send_upper()

    for k in range(HELD, CHUNKS - 1):
        release(k)
    local_step(S1, OB, 0)

    lane_y = lax.broadcasted_iota(jnp.int32, (1, ny), 1)
    keep_first = (lane_y > 0).astype(F32)
    keep_last = (lane_y < ny - 1).astype(F32)
    for j in range(nx):
        both = S1[j, pl.ds(PAD, ny), :] + OB[j]
        BW[j] = turned(pick_wall, both, precision=lax.Precision.HIGHEST)[0:2, :]
        EP[j] = turned(pick_wall.astype(BF16), PB[j])[0:2, :]

    def wall_correct(s):
        w = WR[s].astype(F32)
        t, n, q = w[0:2, :], w[2:4, :], w[4:6, :]
        p = EP[near[s]]
        beside = pltpu.roll(t, 1, 1) * keep_first + pltpu.roll(t, ny - 1, 1) * keep_last
        d = ((3.0 * mobility_step) * (p * p) - mobility_step) * t + q
        d = d - 2.0 * stiffness_step * (n + beside - 6.0 * t)
        BW[near[s]] = BW[near[s]] + d
        BW[far[s]] = BW[far[s]] - stiffness_step * t

    def finish_chunk(k):
        lo, hi = lagged(1, k, 16)
        for s in range(2):
            @pl.when(has[s])
            def _():
                landing(1, s, k, *cuts[1][k]).wait_recv()
                unpack(1, s, *cuts[1][k])
                correct(1, OB, 0, s, lo, hi)

    n_red = GS.shape[0]
    stride = n_cond // n_red
    for s in range(2):
        @pl.when(has[s])
        def _():
            wall_in(s).wait_recv()
            wall_correct(s)
    for j in range(nx):
        p = EP[j]
        g = (1.0 - p * p) * BW[j]
        for w in range(2):
            GS[2 * j + w] = g[w : w + 1, :]

    @pl.when(c > 0)
    def _():
        pl.semaphore_wait(go2, 1)

    def part(r, slot):
        return pltpu.make_async_remote_copy(
            src_ref=GS.at[r], dst_ref=RR.at[slot], send_sem=gs.at[r], recv_sem=gr.at[slot],
            device_id=(r * stride, me), device_id_type=MESH,
        )

    def whole(d, r):
        return pltpu.make_async_remote_copy(
            src_ref=tot, dst_ref=FIN.at[r], send_sem=fs.at[d], recv_sem=fr.at[r],
            device_id=(d, me), device_id_type=MESH,
        )

    for r in range(n_red):
        @pl.when(c != r * stride)
        def _():
            part(r, c).start()

    mine_r = c // stride
    reducer = lax.rem(c, stride) == 0

    release(CHUNKS - 1)

    @pl.when(reducer)
    def _():
        tot[...] = GS[mine_r]

        def add(i, _):
            d = lax.rem(c + i, n_cond)
            part(mine_r, d).wait_recv()
            tot[...] = tot[...] + RR[d]
            return 0
        lax.fori_loop(1, n_cond, add, 0)

        def tell(i, _):
            whole(lax.rem(c + i, n_cond), mine_r).start()
            return 0
        lax.fori_loop(1, n_cond, tell, 0)
        FIN[mine_r] = tot[...]

    for k in range(CHUNKS - 1):
        finish_chunk(k)

    def rows_in(i, _):
        d = lax.rem(me + i, n_slab)
        row_copy(d, d).wait_recv()
        return 0
    lax.fori_loop(1, n_slab, rows_in, 0)
    TA[...] = jnp.zeros_like(TA)
    for i in range(2):
        TA[pl.ds(i * n_slab, n_slab), pl.ds(0, nz)] = RT[:, i, :].astype(BF16)
    TA[:, pl.ds(nz, nz)] = jnp.ones((nz, nz), BF16)
    hi_sum = jnp.sum(RT[:, 2, :].astype(F32), axis=0, keepdims=True)
    lo_sum = jnp.sum(RT[:, 3, :].astype(F32), axis=0, keepdims=True)
    where_to = ((hi_sum - 1.0) * 16.0 + lo_sum).astype(jnp.int32)
    per = ny // nz
    for j in range(nx):
        for b in range(per):
            r = b * nz
            at = lax.broadcasted_iota(jnp.int32, (nz, nz), 0) + (j * ny + r)
            hit = (at == where_to).astype(F32).astype(BF16)
            both = jnp.dot(hit, TA[...], preferred_element_type=F32)
            p = PB[j, pl.ds(r, nz), :].astype(F32)
            OB[j, pl.ds(r, nz), :] = OB[j, pl.ds(r, nz), :] + (p * both[:, nz:] - both[:, :nz])


    finish_chunk(CHUNKS - 1)

    for r in range(n_red):
        @pl.when(c != r * stride)
        def _():
            whole(c, r).wait_recv()
    for w in range(2):
        for x in range(nx):
            grad[w, x : x + 1, :] = (wall_weight * mv[w, x : x + 1, :].astype(F32)) * FIN[2 * x + w]

    for phase in range(2):
        for s in range(2):
            @pl.when(has[s])
            def _():
                for k in range(CHUNKS):
                    piece(phase, s, k, *cuts[phase][k]).wait_send()

    def rows_out(i, _):
        d = lax.rem(me + i, n_slab)
        row_copy(d, me).wait_send()
        return 0
    lax.fori_loop(1, n_slab, rows_out, 0)
    for r in range(n_red):
        @pl.when(c != r * stride)
        def _():
            part(r, c).wait_send()

    @pl.when(reducer)
    def _():
        def sent(i, _):
            whole(lax.rem(c + i, n_cond), mine_r).wait_send()
            return 0
        lax.fori_loop(1, n_cond, sent, 0)
    for s in range(2):
        @pl.when(has[s])
        def _():
            wall_out(s).wait_send()


def deliver(state, walls, out, grad, sem):
    ny = state.shape[2]
    parts = [
        pltpu.make_async_copy(state.at[0, j], out.at[0, j], sem.at[j]) for j in range(state.shape[1])
    ]
    parts.append(pltpu.make_async_copy(walls, grad, sem.at[state.shape[1]]))
    for cp in parts:
        cp.start()
    for cp in parts:
        cp.wait()


def on_device(adjoint, phase, targets, owners, target_cell, rate_index, inflow_rates, wall_mask):
    n_cond = lax.axis_size("cond")
    n_slab = lax.axis_size("slab")
    _, nx, ny, nz = adjoint.shape
    n_rows = targets.shape[1]
    n_red = 2 * nx
    n_rates = inflow_rates.shape[0]
    hbm = pl.BlockSpec(memory_space=pltpu.HBM)
    vmem = pl.BlockSpec(memory_space=pltpu.VMEM)
    dma = pltpu.SemaphoreType.DMA
    padded = ny + 2 * PAD
    call = pl.pallas_call(
        functools.partial(kernel, n_cond, n_slab),
        out_shape=(
            pltpu.VMEM(adjoint.shape, F32),
            pltpu.VMEM(wall_mask.shape, F32),
        ),
        in_specs=[hbm] * 5 + [pl.BlockSpec(memory_space=pltpu.SMEM)] + [hbm] * 2,
        out_specs=(vmem, vmem),
        scratch_shapes=[
            pltpu.VMEM((nx, padded, nz), F32),
            pltpu.VMEM((nx, ny, nz), BF16),
            pltpu.VMEM((nx, padded, nz), F32),
            pltpu.VMEM((nx, padded, nz), F32),
            pltpu.VMEM((2, padded, nz), F32),
            pltpu.VMEM((2, padded, nz), F32),
            pltpu.VMEM((2, 2, 2, ny, nz), BF16),
            pltpu.VMEM((2, 2, 2, ny, nz), BF16),
            pltpu.VMEM((n_rows, nz), BF16),
            pltpu.VMEM((1, n_rows), jnp.int32),
            pltpu.VMEM((1, n_rows), jnp.int32),
            pltpu.VMEM(wall_mask.shape, jnp.int32),
            pltpu.VMEM((1, n_rates), F32),
            pltpu.VMEM((n_slab, 4, nz), ROW),
            pltpu.VMEM((n_slab, 4, nz), ROW),
            pltpu.VMEM((nz, 2 * nz), BF16),
            pltpu.VMEM((nx, 2, ny), F32),
            pltpu.VMEM((nx, 2, ny), F32),
            pltpu.VMEM((2, 8, ny), BF16),
            pltpu.VMEM((2, 8, ny), BF16),
            pltpu.VMEM((n_red, 1, ny), F32),
            pltpu.VMEM((n_cond, 1, ny), F32),
            pltpu.VMEM((n_red, 1, ny), F32),
            pltpu.VMEM((1, ny), F32),
            dma((nx + 6,)),
            dma((2, 2, CHUNKS)),
            dma((2, 2, CHUNKS)),
            dma((n_slab,)),
            dma((n_slab,)),
            dma((n_red,)),
            dma((n_cond,)),
            dma((n_cond,)),
            dma((n_red,)),
            dma((2,)),
            dma((2,)),
            pltpu.SemaphoreType.REGULAR,
            pltpu.SemaphoreType.REGULAR,
            pltpu.SemaphoreType.REGULAR,
        ],
        compiler_params=pltpu.CompilerParams(
            collective_id=0, has_side_effects=True, vmem_limit_bytes=56 * 1024 * 1024
        ),
    )
    owner_row = owners.reshape(1, n_rows)
    state, walls = call(
        adjoint, phase, targets, owner_row, target_cell,
        rate_index, inflow_rates.reshape(1, n_rates), wall_mask,
    )
    return pl.pallas_call(
        deliver,
        out_shape=(
            jax.ShapeDtypeStruct(adjoint.shape, F32),
            jax.ShapeDtypeStruct(wall_mask.shape, F32),
        ),
        in_specs=[pl.BlockSpec(memory_space=pl.ANY)] * 2,
        out_specs=(hbm, hbm),
        scratch_shapes=[dma((nx + 1,))],
        compiler_params=pltpu.CompilerParams(vmem_limit_bytes=4 * 1024 * 1024),
    )(state, walls)


ROW = BF16


def solution(mesh):
    in_specs = (
        P("cond", "slab", None, None),
        P("cond", "slab", None, None),
        P("cond", "slab", None),
        P("cond", "slab", None),
        P("cond", "slab"),
        P("cond"),
        P(),
        P(None, "slab", None),
    )
    out_specs = (P("cond", "slab", None, None), P(None, "slab", None))
    return jax.shard_map(
        on_device, mesh=mesh, in_specs=in_specs, out_specs=out_specs, check_vma=False
    )
```

```python
import functools

import jax
import jax.numpy as jnp
from jax import lax
from jax.experimental import pallas as pl
from jax.experimental.pallas import tpu as pltpu
from jax.sharding import PartitionSpec as P

MESH = pl.DeviceIdType.MESH
F32 = jnp.float32
BF16 = jnp.bfloat16

mobility_step = 0.02
stiffness_step = 0.01
transport_step = 0.125
wall_weight = 0.25

CHUNKS = 4
HELD = 1
PAD = 8


def kernel(
    n_cond, n_slab, adj, ph, tgt, own, cell, ridx, rates, mask, out, grad,
    S, PB, F, S1, H, LO, SB, RB, tv, ov, cv, mv, fv, ST, RT, TA, BW, EP, WS, WR, GS, RR, FIN, tot,
    in_sem, ss, rs, ts, tr, gs, gr, fs, fr, ws, wr, go, go2, up,
):
    OB = out.at[0]
    ny = S.shape[1] - 2 * PAD
    nz = S.shape[2]
    nx = S.shape[0]
    c = lax.axis_index("cond")
    me = lax.axis_index("slab")
    last = n_slab - 1
    has = (me > 0, me < last)
    peer = (me - 1, me + 1)
    near = (0, nx - 1)
    far = (1, nx - 2)
    step = ny // CHUNKS

    loads = [pltpu.make_async_copy(adj.at[0, j], S.at[j, pl.ds(PAD, ny)], in_sem.at[j]) for j in range(nx)]
    ph_load = pltpu.make_async_copy(ph.at[0], PB, in_sem.at[nx])
    small = [
        pltpu.make_async_copy(tgt.at[0], tv, in_sem.at[nx + 1]),
        pltpu.make_async_copy(own, ov, in_sem.at[nx + 2]),
        pltpu.make_async_copy(cell, cv, in_sem.at[nx + 3]),
        pltpu.make_async_copy(mask, mv, in_sem.at[nx + 4]),
        pltpu.make_async_copy(rates, fv, in_sem.at[nx + 5]),
    ]
    for j in (0, nx - 1, 1, nx - 2):
        loads[j].start()
    for cp in small:
        cp.start()
    ph_load.start()

    bar = pltpu.get_barrier_semaphore()
    for s in range(2):
        @pl.when(has[s])
        def _():
            pl.semaphore_signal(bar, inc=1, device_id=(c, peer[s]), device_id_type=MESH)

    half = n_slab // 2
    upper = me >= half
    hub = jnp.where(upper, last, half - 1)

    @pl.when(me < hub - 1)
    def _():
        pl.semaphore_signal(bar, inc=1, device_id=(c, hub), device_id_type=MESH)

    @pl.when(c > 0)
    def _():
        pl.semaphore_signal(bar, inc=1, device_id=(0, me), device_id_type=MESH)

    @pl.when(jnp.logical_not(upper))
    def _():
        def greet(d, _):
            pl.semaphore_signal(bar, inc=1, device_id=(c, d), device_id_type=MESH)
            return 0
        lax.fori_loop(jnp.where(me == half - 1, half + 1, half), n_slab, greet, 0)

    lane = lax.broadcasted_iota(jnp.int32, (1, nz), 1)
    keep_lo = (lane > 0).astype(F32)
    keep_hi = (lane < nz - 1).astype(F32)
    height = (lane.astype(F32) + 0.5) / nz
    profile = 4.0 * height * (1.0 - height)

    def in_plane(ref, j, r, n):
        x = ref[j, pl.ds(r + PAD, n), :]
        zsum = pltpu.roll(x, 1, 1) * keep_lo + pltpu.roll(x, nz - 1, 1) * keep_hi
        return zsum + ref[j, pl.ds(r + (PAD - 1), n), :] + ref[j, pl.ds(r + (PAD + 1), n), :] - 6.0 * x

    def rows(lo, hi, body):
        r = lo
        while r < hi:
            n = min(64, hi - r)
            body(r, n)
            r += n

    def mobility(j, r, n):
        p = PB[j, pl.ds(r, n), :].astype(F32)
        return (3.0 * mobility_step) * (p * p) - mobility_step

    zpad = jnp.zeros((PAD, nz), F32)
    for ref in (S, F, S1):
        for j in range(nx):
            ref[j, pl.ds(0, PAD), :] = zpad
            ref[j, pl.ds(PAD + ny, PAD), :] = zpad
    for ref in (H, LO):
        for j in range(2):
            ref[j, pl.ds(0, PAD), :] = zpad
            ref[j, pl.ds(PAD + ny, PAD), :] = zpad

    def split(ref, phase, s, lo, hi):
        def body(r, n):
            x = ref[near[s], pl.ds(r + PAD, n), :]
            h = x.astype(BF16)
            SB[phase, s, 0, pl.ds(r, n), :] = h
            LO[s, pl.ds(r + PAD, n), :] = x - h.astype(F32)
        rows(lo, hi, body)

    def residue(ref, phase, s, lo, hi):
        def body(r, n):
            q = -2.0 * stiffness_step * in_plane(LO, s, r, n) - stiffness_step * ref[far[s], pl.ds(r + PAD, n), :]
            SB[phase, s, 1, pl.ds(r, n), :] = q.astype(BF16)
        rows(lo, hi, body)

    def piece(phase, s, k, lo, hi):
        return pltpu.make_async_remote_copy(
            src_ref=SB.at[phase, s, :, pl.ds(lo, hi - lo)],
            dst_ref=RB.at[phase, 1 - s, :, pl.ds(lo, hi - lo)],
            send_sem=ss.at[phase, s, k],
            recv_sem=rs.at[phase, 1 - s, k],
            device_id=(c, peer[s]),
            device_id_type=MESH,
        )

    def landing(phase, s, k, lo, hi):
        return pltpu.make_async_remote_copy(
            src_ref=SB.at[phase, 1 - s, :, pl.ds(lo, hi - lo)],
            dst_ref=RB.at[phase, s, :, pl.ds(lo, hi - lo)],
            send_sem=ss.at[phase, 1 - s, k],
            recv_sem=rs.at[phase, s, k],
            device_id=(c, peer[s]),
            device_id_type=MESH,
        )

    cuts = [[(k * step, (k + 1) * step) for k in range(CHUNKS)]]
    for lag in (32,):
        edges = [0] + [k * step - lag for k in range(1, CHUNKS)] + [ny]
        cuts.append(list(zip(edges[:-1], edges[1:])))

    def lagged(phase, k, lag):
        lo = 0 if k == 0 else cuts[phase][k][0] - lag
        hi = ny if k == CHUNKS - 1 else cuts[phase][k][1] - lag
        return lo, hi

    for s in range(2):
        loads[near[s]].wait()
        split(S, 0, s, 0, ny)
        loads[far[s]].wait()
        residue(S, 0, s, 0, ny)

    greeted = has[0].astype(jnp.int32) + has[1].astype(jnp.int32)
    greeted = greeted + jnp.where(me == hub, half - 2, 0) + jnp.where(c == 0, n_cond - 1, 0)
    greeted = greeted + jnp.where(upper, half, 0) - jnp.where(me == half, 1, 0)
    pl.semaphore_wait(bar, greeted)
    for s in range(2):
        @pl.when(has[s])
        def _():
            piece(0, s, 0, *cuts[0][0]).start()

    for cp in small:
        cp.wait()
    entry = lax.broadcasted_iota(jnp.int32, fv.shape, 1)
    inflow = jnp.sum(jnp.where(entry == ridx[0], fv[...], 0.0), axis=1, keepdims=True)
    drift = (transport_step * inflow) * profile
    n_rows = tv.shape[0]
    match = (ov[...] == lax.broadcasted_iota(jnp.int32, (n_slab, n_rows), 0)).astype(F32)
    prior = (
        lax.broadcasted_iota(jnp.int32, (n_rows, n_rows), 0) < lax.broadcasted_iota(jnp.int32, (n_rows, n_rows), 1)
    ).astype(BF16)
    earlier = jnp.dot(match.astype(BF16), prior, preferred_element_type=F32)
    first = jnp.where(earlier < 0.5, match, 0.0)
    second = match - first
    code = cv[...].astype(F32) + 16.0
    lanes = lax.broadcasted_iota(jnp.int32, (n_slab, nz), 1)
    high = jnp.zeros((n_slab, nz), F32)
    low = jnp.zeros((n_slab, nz), F32)
    for i, pick in enumerate((first, second)):
        ST[:, i, :] = jnp.dot(pick.astype(BF16), tv[...], preferred_element_type=F32).astype(ST.dtype)
        mine = jnp.sum(pick * code, axis=1, keepdims=True)
        hi_part = jnp.floor(mine * (1.0 / 16.0))
        here = lanes == me + i * n_slab
        high = jnp.where(here, hi_part, high)
        low = jnp.where(here, mine - 16.0 * hi_part, low)
    ST[:, 2, :] = high.astype(ST.dtype)
    ST[:, 3, :] = low.astype(ST.dtype)
    RT[me] = ST[me]

    def row_copy(d, slot):
        return pltpu.make_async_remote_copy(
            src_ref=ST.at[d], dst_ref=RT.at[slot], send_sem=ts.at[d], recv_sem=tr.at[slot],
            device_id=(c, d), device_id_type=MESH,
        )

    @pl.when(upper)
    def _():
        def one(d, _):
            row_copy(d, me).start()
            return 0
        lax.fori_loop(0, half, one, 0)
    for k in range(1, CHUNKS):
        for s in range(2):
            @pl.when(has[s])
            def _():
                piece(0, s, k, *cuts[0][k]).start()

    @pl.when(me == hub)
    def _():
        def tell(i, _):
            pl.semaphore_signal(go, inc=1, device_id=(c, me - i), device_id_type=MESH)
            return 0
        lax.fori_loop(1, half, tell, 0)

    @pl.when(upper)
    def _():
        def tell(d, _):
            pl.semaphore_signal(up, inc=1, device_id=(c, d), device_id_type=MESH)
            return 0
        lax.fori_loop(0, half, tell, 0)

    @pl.when(c == 0)
    def _():
        def tell(d, _):
            pl.semaphore_signal(go2, inc=1, device_id=(d, me), device_id_type=MESH)
            return 0
        lax.fori_loop(1, n_cond, tell, 0)

    first_own = jnp.where(upper, half, 0)

    def send_own_half():
        @pl.when(me != hub)
        def _():
            pl.semaphore_wait(go, 1)

        def one(i, _):
            row_copy(first_own + lax.rem(me - first_own + i, half), me).start()
            return 0
        lax.fori_loop(1, half, one, 0)

    def send_upper():
        pl.semaphore_wait(up, n_slab - half)

        def one(d, _):
            row_copy(d, me).start()
            return 0
        lax.fori_loop(half, n_slab, one, 0)

    ghost = (has[0].astype(F32), has[1].astype(F32))

    def local_step(src, dst, padded):
        def laps(r, n):
            for j in range(nx):
                v = in_plane(src, j, r, n)
                for o in (j - 1, j + 1):
                    if 0 <= o < nx:
                        v = v + src[o, pl.ds(r + PAD, n), :]
                F[j, pl.ds(r + PAD, n), :] = v
        rows(0, ny, laps)

        def update(r, n):
            for j in range(nx):
                lap2 = in_plane(F, j, r, n)
                for o in (j - 1, j + 1):
                    if 0 <= o < nx:
                        lap2 = lap2 + F[o, pl.ds(r + PAD, n), :]
                x = src[j, pl.ds(r + PAD, n), :]
                for s in range(2):
                    if j == near[s]:
                        lap2 = lap2 + ghost[s] * x
                moved = src[j, pl.ds(r + (PAD + 1), n), :] - src[j, pl.ds(r + (PAD - 1), n), :]
                v = x + mobility(j, r, n) * F[j, pl.ds(r + PAD, n), :] - stiffness_step * lap2 + drift * moved
                dst[j, pl.ds(r + padded, n), :] = v
        rows(0, ny, update)

    def unpack(phase, s, lo, hi):
        def body(r, n):
            H[s, pl.ds(r + PAD, n), :] = RB[phase, s, 0, pl.ds(r, n), :].astype(F32)
        rows(lo, hi, body)

    def correct(phase, dst, padded, s, lo, hi):
        def body(r, n):
            h = H[s, pl.ds(r + PAD, n), :]
            v = dst[near[s], pl.ds(r + padded, n), :] + mobility(near[s], r, n) * h
            v = v - 2.0 * stiffness_step * in_plane(H, s, r, n) + RB[phase, s, 1, pl.ds(r, n), :].astype(F32)
            dst[near[s], pl.ds(r + padded, n), :] = v
            dst[far[s], pl.ds(r + padded, n), :] = dst[far[s], pl.ds(r + padded, n), :] - stiffness_step * h
        rows(lo, hi, body)

    def chosen(places):
        row = lax.broadcasted_iota(jnp.int32, (8, nz), 0)
        col = lax.broadcasted_iota(jnp.int32, (8, nz), 1)
        pick = jnp.zeros((8, nz), F32)
        for i, z in places:
            pick = jnp.where(jnp.logical_and(row == i, col == z), 1.0, pick)
        return pick

    def turned(pick, x, **kw):
        return lax.dot_general(pick, x, (((1,), (1,)), ((), ())), preferred_element_type=F32, **kw)

    pick_wall = chosen(((0, 0), (1, nz - 1)))
    pick_t = chosen(((0, 0), (1, nz - 1), (2, 1), (3, nz - 2))).astype(BF16)
    pick_q = chosen(((4, 0), (5, nz - 1))).astype(BF16)

    def wall_lanes(s):
        WS[s] = (turned(pick_t, SB[1, s, 0]) + turned(pick_q, SB[1, s, 1])).astype(BF16)

    def wall_out(s):
        return pltpu.make_async_remote_copy(
            src_ref=WS.at[s], dst_ref=WR.at[1 - s], send_sem=ws.at[s], recv_sem=wr.at[1 - s],
            device_id=(c, peer[s]), device_id_type=MESH,
        )

    def wall_in(s):
        return pltpu.make_async_remote_copy(
            src_ref=WS.at[1 - s], dst_ref=WR.at[s], send_sem=ws.at[1 - s], recv_sem=wr.at[s],
            device_id=(c, peer[s]), device_id_type=MESH,
        )

    ph_load.wait()
    local_step(S, S1, PAD)
    for k in range(CHUNKS):
        for s in range(2):
            @pl.when(has[s])
            def _():
                landing(0, s, k, *cuts[0][k]).wait_recv()
                unpack(0, s, *cuts[0][k])
                lo, hi = lagged(0, k, 16)
                correct(0, S1, PAD, s, lo, hi)
                split(S1, 1, s, lo, hi)
                residue(S1, 1, s, *cuts[1][k])
                if k < HELD:
                    piece(1, s, k, *cuts[1][k]).start()
                if k == CHUNKS - 1:
                    wall_lanes(s)
                    wall_out(s).start()
        if k == 1:
            send_own_half()

    def release(k):
        for s in range(2):
            @pl.when(has[s])
            def _():
                piece(1, s, k, *cuts[1][k]).start()

    @pl.when(jnp.logical_not(upper))
    def _():
        send_upper()

    for k in range(HELD, CHUNKS - 1):
        release(k)
    local_step(S1, OB, 0)

    lane_y = lax.broadcasted_iota(jnp.int32, (1, ny), 1)
    keep_first = (lane_y > 0).astype(F32)
    keep_last = (lane_y < ny - 1).astype(F32)
    for j in range(nx):
        both = S1[j, pl.ds(PAD, ny), :] + OB[j]
        BW[j] = turned(pick_wall, both, precision=lax.Precision.HIGHEST)[0:2, :]
        EP[j] = turned(pick_wall.astype(BF16), PB[j])[0:2, :]

    def wall_correct(s):
        w = WR[s].astype(F32)
        t, n, q = w[0:2, :], w[2:4, :], w[4:6, :]
        p = EP[near[s]]
        beside = pltpu.roll(t, 1, 1) * keep_first + pltpu.roll(t, ny - 1, 1) * keep_last
        d = ((3.0 * mobility_step) * (p * p) - mobility_step) * t + q
        d = d - 2.0 * stiffness_step * (n + beside - 6.0 * t)
        BW[near[s]] = BW[near[s]] + d
        BW[far[s]] = BW[far[s]] - stiffness_step * t

    def finish_chunk(k):
        lo, hi = lagged(1, k, 16)
        for s in range(2):
            @pl.when(has[s])
            def _():
                landing(1, s, k, *cuts[1][k]).wait_recv()
                unpack(1, s, *cuts[1][k])
                correct(1, OB, 0, s, lo, hi)

    n_red = GS.shape[0]
    stride = n_cond // n_red
    for s in range(2):
        @pl.when(has[s])
        def _():
            wall_in(s).wait_recv()
            wall_correct(s)
    for j in range(nx):
        p = EP[j]
        g = (1.0 - p * p) * BW[j]
        for w in range(2):
            GS[2 * j + w] = g[w : w + 1, :]

    @pl.when(c > 0)
    def _():
        pl.semaphore_wait(go2, 1)

    def part(r, slot):
        return pltpu.make_async_remote_copy(
            src_ref=GS.at[r], dst_ref=RR.at[slot], send_sem=gs.at[r], recv_sem=gr.at[slot],
            device_id=(r * stride, me), device_id_type=MESH,
        )

    def whole(d, r):
        return pltpu.make_async_remote_copy(
            src_ref=tot, dst_ref=FIN.at[r], send_sem=fs.at[d], recv_sem=fr.at[r],
            device_id=(d, me), device_id_type=MESH,
        )

    for r in range(n_red):
        @pl.when(c != r * stride)
        def _():
            part(r, c).start()

    mine_r = c // stride
    reducer = lax.rem(c, stride) == 0

    release(CHUNKS - 1)
    for k in range(CHUNKS - 2):
        finish_chunk(k)

    @pl.when(reducer)
    def _():
        tot[...] = GS[mine_r]

        def add(i, _):
            d = lax.rem(c + i, n_cond)
            part(mine_r, d).wait_recv()
            tot[...] = tot[...] + RR[d]
            return 0
        lax.fori_loop(1, n_cond, add, 0)

        def tell(i, _):
            whole(lax.rem(c + i, n_cond), mine_r).start()
            return 0
        lax.fori_loop(1, n_cond, tell, 0)
        FIN[mine_r] = tot[...]

    finish_chunk(CHUNKS - 2)

    def rows_in(i, _):
        d = lax.rem(me + i, n_slab)
        row_copy(d, d).wait_recv()
        return 0
    lax.fori_loop(1, n_slab, rows_in, 0)
    TA[...] = jnp.zeros_like(TA)
    for i in range(2):
        TA[pl.ds(i * n_slab, n_slab), pl.ds(0, nz)] = RT[:, i, :].astype(BF16)
    TA[:, pl.ds(nz, nz)] = jnp.ones((nz, nz), BF16)
    hi_sum = jnp.sum(RT[:, 2, :].astype(F32), axis=0, keepdims=True)
    lo_sum = jnp.sum(RT[:, 3, :].astype(F32), axis=0, keepdims=True)
    where_to = ((hi_sum - 1.0) * 16.0 + lo_sum).astype(jnp.int32)
    per = ny // nz
    for j in range(nx):
        for b in range(per):
            r = b * nz
            at = lax.broadcasted_iota(jnp.int32, (nz, nz), 0) + (j * ny + r)
            hit = (at == where_to).astype(F32).astype(BF16)
            both = jnp.dot(hit, TA[...], preferred_element_type=F32)
            p = PB[j, pl.ds(r, nz), :].astype(F32)
            OB[j, pl.ds(r, nz), :] = OB[j, pl.ds(r, nz), :] + (p * both[:, nz:] - both[:, :nz])


    finish_chunk(CHUNKS - 1)

    for r in range(n_red):
        @pl.when(c != r * stride)
        def _():
            whole(c, r).wait_recv()
    for w in range(2):
        for x in range(nx):
            grad[w, x : x + 1, :] = (wall_weight * mv[w, x : x + 1, :].astype(F32)) * FIN[2 * x + w]

    for phase in range(2):
        for s in range(2):
            @pl.when(has[s])
            def _():
                for k in range(CHUNKS):
                    piece(phase, s, k, *cuts[phase][k]).wait_send()

    def rows_out(i, _):
        d = lax.rem(me + i, n_slab)
        row_copy(d, me).wait_send()
        return 0
    lax.fori_loop(1, n_slab, rows_out, 0)
    for r in range(n_red):
        @pl.when(c != r * stride)
        def _():
            part(r, c).wait_send()

    @pl.when(reducer)
    def _():
        def sent(i, _):
            whole(lax.rem(c + i, n_cond), mine_r).wait_send()
            return 0
        lax.fori_loop(1, n_cond, sent, 0)
    for s in range(2):
        @pl.when(has[s])
        def _():
            wall_out(s).wait_send()


def deliver(state, walls, out, grad, sem):
    ny = state.shape[2]
    parts = [
        pltpu.make_async_copy(state.at[0, j], out.at[0, j], sem.at[j]) for j in range(state.shape[1])
    ]
    parts.append(pltpu.make_async_copy(walls, grad, sem.at[state.shape[1]]))
    for cp in parts:
        cp.start()
    for cp in parts:
        cp.wait()


def on_device(adjoint, phase, targets, owners, target_cell, rate_index, inflow_rates, wall_mask):
    n_cond = lax.axis_size("cond")
    n_slab = lax.axis_size("slab")
    _, nx, ny, nz = adjoint.shape
    n_rows = targets.shape[1]
    n_red = 2 * nx
    n_rates = inflow_rates.shape[0]
    hbm = pl.BlockSpec(memory_space=pltpu.HBM)
    vmem = pl.BlockSpec(memory_space=pltpu.VMEM)
    dma = pltpu.SemaphoreType.DMA
    padded = ny + 2 * PAD
    call = pl.pallas_call(
        functools.partial(kernel, n_cond, n_slab),
        out_shape=(
            pltpu.VMEM(adjoint.shape, F32),
            pltpu.VMEM(wall_mask.shape, F32),
        ),
        in_specs=[hbm] * 5 + [pl.BlockSpec(memory_space=pltpu.SMEM)] + [hbm] * 2,
        out_specs=(vmem, vmem),
        scratch_shapes=[
            pltpu.VMEM((nx, padded, nz), F32),
            pltpu.VMEM((nx, ny, nz), BF16),
            pltpu.VMEM((nx, padded, nz), F32),
            pltpu.VMEM((nx, padded, nz), F32),
            pltpu.VMEM((2, padded, nz), F32),
            pltpu.VMEM((2, padded, nz), F32),
            pltpu.VMEM((2, 2, 2, ny, nz), BF16),
            pltpu.VMEM((2, 2, 2, ny, nz), BF16),
            pltpu.VMEM((n_rows, nz), BF16),
            pltpu.VMEM((1, n_rows), jnp.int32),
            pltpu.VMEM((1, n_rows), jnp.int32),
            pltpu.VMEM(wall_mask.shape, jnp.int32),
            pltpu.VMEM((1, n_rates), F32),
            pltpu.VMEM((n_slab, 4, nz), ROW),
            pltpu.VMEM((n_slab, 4, nz), ROW),
            pltpu.VMEM((nz, 2 * nz), BF16),
            pltpu.VMEM((nx, 2, ny), F32),
            pltpu.VMEM((nx, 2, ny), F32),
            pltpu.VMEM((2, 8, ny), BF16),
            pltpu.VMEM((2, 8, ny), BF16),
            pltpu.VMEM((n_red, 1, ny), F32),
            pltpu.VMEM((n_cond, 1, ny), F32),
            pltpu.VMEM((n_red, 1, ny), F32),
            pltpu.VMEM((1, ny), F32),
            dma((nx + 6,)),
            dma((2, 2, CHUNKS)),
            dma((2, 2, CHUNKS)),
            dma((n_slab,)),
            dma((n_slab,)),
            dma((n_red,)),
            dma((n_cond,)),
            dma((n_cond,)),
            dma((n_red,)),
            dma((2,)),
            dma((2,)),
            pltpu.SemaphoreType.REGULAR,
            pltpu.SemaphoreType.REGULAR,
            pltpu.SemaphoreType.REGULAR,
        ],
        compiler_params=pltpu.CompilerParams(
            collective_id=0, has_side_effects=True, vmem_limit_bytes=56 * 1024 * 1024
        ),
    )
    owner_row = owners.reshape(1, n_rows)
    state, walls = call(
        adjoint, phase, targets, owner_row, target_cell,
        rate_index, inflow_rates.reshape(1, n_rates), wall_mask,
    )
    return pl.pallas_call(
        deliver,
        out_shape=(
            jax.ShapeDtypeStruct(adjoint.shape, F32),
            jax.ShapeDtypeStruct(wall_mask.shape, F32),
        ),
        in_specs=[pl.BlockSpec(memory_space=pl.ANY)] * 2,
        out_specs=(hbm, hbm),
        scratch_shapes=[dma((nx + 1,))],
        compiler_params=pltpu.CompilerParams(vmem_limit_bytes=4 * 1024 * 1024),
    )(state, walls)


ROW = BF16


def solution(mesh):
    in_specs = (
        P("cond", "slab", None, None),
        P("cond", "slab", None, None),
        P("cond", "slab", None),
        P("cond", "slab", None),
        P("cond", "slab"),
        P("cond"),
        P(),
        P(None, "slab", None),
    )
    out_specs = (P("cond", "slab", None, None), P(None, "slab", None))
    return jax.shard_map(
        on_device, mesh=mesh, in_specs=in_specs, out_specs=out_specs, check_vma=False
    )
```

```python
import functools

import jax
import jax.numpy as jnp
from jax import lax
from jax.experimental import pallas as pl
from jax.experimental.pallas import tpu as pltpu
from jax.sharding import PartitionSpec as P

MESH = pl.DeviceIdType.MESH
F32 = jnp.float32
BF16 = jnp.bfloat16

mobility_step = 0.02
stiffness_step = 0.01
transport_step = 0.125
wall_weight = 0.25

CHUNKS = 4
HELD = 1
PAD = 8


def kernel(
    n_cond, n_slab, adj, ph, tgt, own, cell, ridx, rates, mask, out, grad,
    S, PB, F, S1, H, LO, SB, RB, tv, ov, cv, mv, fv, ST, RT, TA, BW, EP, WS, WR, GS, RR, FIN, tot,
    in_sem, ss, rs, ts, tr, gs, gr, fs, fr, ws, wr, go, go2, up,
):
    OB = out.at[0]
    ny = S.shape[1] - 2 * PAD
    nz = S.shape[2]
    nx = S.shape[0]
    c = lax.axis_index("cond")
    me = lax.axis_index("slab")
    last = n_slab - 1
    has = (me > 0, me < last)
    peer = (me - 1, me + 1)
    near = (0, nx - 1)
    far = (1, nx - 2)
    step = ny // CHUNKS

    loads = [pltpu.make_async_copy(adj.at[0, j], S.at[j, pl.ds(PAD, ny)], in_sem.at[j]) for j in range(nx)]
    ph_load = pltpu.make_async_copy(ph.at[0], PB, in_sem.at[nx])
    small = [
        pltpu.make_async_copy(tgt.at[0], tv, in_sem.at[nx + 1]),
        pltpu.make_async_copy(own, ov, in_sem.at[nx + 2]),
        pltpu.make_async_copy(cell, cv, in_sem.at[nx + 3]),
        pltpu.make_async_copy(mask, mv, in_sem.at[nx + 4]),
        pltpu.make_async_copy(rates, fv, in_sem.at[nx + 5]),
    ]
    for j in (0, nx - 1, 1, nx - 2):
        loads[j].start()
    for cp in small:
        cp.start()
    ph_load.start()

    bar = pltpu.get_barrier_semaphore()
    for s in range(2):
        @pl.when(has[s])
        def _():
            pl.semaphore_signal(bar, inc=1, device_id=(c, peer[s]), device_id_type=MESH)

    half = n_slab // 2
    upper = me >= half
    hub = jnp.where(upper, last, half - 1)

    @pl.when(me < hub - 1)
    def _():
        pl.semaphore_signal(bar, inc=1, device_id=(c, hub), device_id_type=MESH)

    @pl.when(c > 0)
    def _():
        pl.semaphore_signal(bar, inc=1, device_id=(0, me), device_id_type=MESH)

    @pl.when(jnp.logical_not(upper))
    def _():
        def greet(d, _):
            pl.semaphore_signal(bar, inc=1, device_id=(c, d), device_id_type=MESH)
            return 0
        lax.fori_loop(jnp.where(me == half - 1, half + 1, half), n_slab, greet, 0)

    lane = lax.broadcasted_iota(jnp.int32, (1, nz), 1)
    keep_lo = (lane > 0).astype(F32)
    keep_hi = (lane < nz - 1).astype(F32)
    height = (lane.astype(F32) + 0.5) / nz
    profile = 4.0 * height * (1.0 - height)

    def in_plane(ref, j, r, n):
        x = ref[j, pl.ds(r + PAD, n), :]
        zsum = pltpu.roll(x, 1, 1) * keep_lo + pltpu.roll(x, nz - 1, 1) * keep_hi
        return zsum + ref[j, pl.ds(r + (PAD - 1), n), :] + ref[j, pl.ds(r + (PAD + 1), n), :] - 6.0 * x

    def rows(lo, hi, body):
        r = lo
        while r < hi:
            n = min(64, hi - r)
            body(r, n)
            r += n

    def mobility(j, r, n):
        p = PB[j, pl.ds(r, n), :].astype(F32)
        return (3.0 * mobility_step) * (p * p) - mobility_step

    zpad = jnp.zeros((PAD, nz), F32)
    for ref in (S, F, S1):
        for j in range(nx):
            ref[j, pl.ds(0, PAD), :] = zpad
            ref[j, pl.ds(PAD + ny, PAD), :] = zpad
    for ref in (H, LO):
        for j in range(2):
            ref[j, pl.ds(0, PAD), :] = zpad
            ref[j, pl.ds(PAD + ny, PAD), :] = zpad

    def split(ref, phase, s, lo, hi):
        def body(r, n):
            x = ref[near[s], pl.ds(r + PAD, n), :]
            h = x.astype(BF16)
            SB[phase, s, 0, pl.ds(r, n), :] = h
            LO[s, pl.ds(r + PAD, n), :] = x - h.astype(F32)
        rows(lo, hi, body)

    def residue(ref, phase, s, lo, hi):
        def body(r, n):
            q = -2.0 * stiffness_step * in_plane(LO, s, r, n) - stiffness_step * ref[far[s], pl.ds(r + PAD, n), :]
            SB[phase, s, 1, pl.ds(r, n), :] = q.astype(BF16)
        rows(lo, hi, body)

    def piece(phase, s, k, lo, hi):
        return pltpu.make_async_remote_copy(
            src_ref=SB.at[phase, s, :, pl.ds(lo, hi - lo)],
            dst_ref=RB.at[phase, 1 - s, :, pl.ds(lo, hi - lo)],
            send_sem=ss.at[phase, s, k],
            recv_sem=rs.at[phase, 1 - s, k],
            device_id=(c, peer[s]),
            device_id_type=MESH,
        )

    def landing(phase, s, k, lo, hi):
        return pltpu.make_async_remote_copy(
            src_ref=SB.at[phase, 1 - s, :, pl.ds(lo, hi - lo)],
            dst_ref=RB.at[phase, s, :, pl.ds(lo, hi - lo)],
            send_sem=ss.at[phase, 1 - s, k],
            recv_sem=rs.at[phase, s, k],
            device_id=(c, peer[s]),
            device_id_type=MESH,
        )

    cuts = [[(k * step, (k + 1) * step) for k in range(CHUNKS)]]
    for lag in (32,):
        edges = [0] + [k * step - lag for k in range(1, CHUNKS)] + [ny]
        cuts.append(list(zip(edges[:-1], edges[1:])))

    def lagged(phase, k, lag):
        lo = 0 if k == 0 else cuts[phase][k][0] - lag
        hi = ny if k == CHUNKS - 1 else cuts[phase][k][1] - lag
        return lo, hi

    for s in range(2):
        loads[near[s]].wait()
        split(S, 0, s, 0, step + 16)
        loads[far[s]].wait()
        residue(S, 0, s, 0, step)

    greeted = has[0].astype(jnp.int32) + has[1].astype(jnp.int32)
    greeted = greeted + jnp.where(me == hub, half - 2, 0) + jnp.where(c == 0, n_cond - 1, 0)
    greeted = greeted + jnp.where(upper, half, 0) - jnp.where(me == half, 1, 0)
    pl.semaphore_wait(bar, greeted)
    for s in range(2):
        @pl.when(has[s])
        def _():
            piece(0, s, 0, *cuts[0][0]).start()

    for s in range(2):
        split(S, 0, s, step + 16, ny)
        residue(S, 0, s, step, ny)

    for cp in small:
        cp.wait()
    entry = lax.broadcasted_iota(jnp.int32, fv.shape, 1)
    inflow = jnp.sum(jnp.where(entry == ridx[0], fv[...], 0.0), axis=1, keepdims=True)
    drift = (transport_step * inflow) * profile
    n_rows = tv.shape[0]
    match = (ov[...] == lax.broadcasted_iota(jnp.int32, (n_slab, n_rows), 0)).astype(F32)
    prior = (
        lax.broadcasted_iota(jnp.int32, (n_rows, n_rows), 0) < lax.broadcasted_iota(jnp.int32, (n_rows, n_rows), 1)
    ).astype(BF16)
    earlier = jnp.dot(match.astype(BF16), prior, preferred_element_type=F32)
    first = jnp.where(earlier < 0.5, match, 0.0)
    second = match - first
    code = cv[...].astype(F32) + 16.0
    lanes = lax.broadcasted_iota(jnp.int32, (n_slab, nz), 1)
    high = jnp.zeros((n_slab, nz), F32)
    low = jnp.zeros((n_slab, nz), F32)
    for i, pick in enumerate((first, second)):
        ST[:, i, :] = jnp.dot(pick.astype(BF16), tv[...], preferred_element_type=F32).astype(ST.dtype)
        mine = jnp.sum(pick * code, axis=1, keepdims=True)
        hi_part = jnp.floor(mine * (1.0 / 16.0))
        here = lanes == me + i * n_slab
        high = jnp.where(here, hi_part, high)
        low = jnp.where(here, mine - 16.0 * hi_part, low)
    ST[:, 2, :] = high.astype(ST.dtype)
    ST[:, 3, :] = low.astype(ST.dtype)
    RT[me] = ST[me]

    def row_copy(d, slot):
        return pltpu.make_async_remote_copy(
            src_ref=ST.at[d], dst_ref=RT.at[slot], send_sem=ts.at[d], recv_sem=tr.at[slot],
            device_id=(c, d), device_id_type=MESH,
        )

    @pl.when(upper)
    def _():
        def one(d, _):
            row_copy(d, me).start()
            return 0
        lax.fori_loop(0, half, one, 0)
    for k in range(1, CHUNKS):
        for s in range(2):
            @pl.when(has[s])
            def _():
                piece(0, s, k, *cuts[0][k]).start()

    @pl.when(me == hub)
    def _():
        def tell(i, _):
            pl.semaphore_signal(go, inc=1, device_id=(c, me - i), device_id_type=MESH)
            return 0
        lax.fori_loop(1, half, tell, 0)

    @pl.when(upper)
    def _():
        def tell(d, _):
            pl.semaphore_signal(up, inc=1, device_id=(c, d), device_id_type=MESH)
            return 0
        lax.fori_loop(0, half, tell, 0)

    @pl.when(c == 0)
    def _():
        def tell(d, _):
            pl.semaphore_signal(go2, inc=1, device_id=(d, me), device_id_type=MESH)
            return 0
        lax.fori_loop(1, n_cond, tell, 0)

    first_own = jnp.where(upper, half, 0)

    def send_own_half():
        @pl.when(me != hub)
        def _():
            pl.semaphore_wait(go, 1)

        def one(i, _):
            row_copy(first_own + lax.rem(me - first_own + i, half), me).start()
            return 0
        lax.fori_loop(1, half, one, 0)

    def send_upper():
        pl.semaphore_wait(up, n_slab - half)

        def one(d, _):
            row_copy(d, me).start()
            return 0
        lax.fori_loop(half, n_slab, one, 0)

    ghost = (has[0].astype(F32), has[1].astype(F32))

    def local_step(src, dst, padded):
        def laps(r, n):
            for j in range(nx):
                v = in_plane(src, j, r, n)
                for o in (j - 1, j + 1):
                    if 0 <= o < nx:
                        v = v + src[o, pl.ds(r + PAD, n), :]
                F[j, pl.ds(r + PAD, n), :] = v
        rows(0, ny, laps)

        def update(r, n):
            for j in range(nx):
                lap2 = in_plane(F, j, r, n)
                for o in (j - 1, j + 1):
                    if 0 <= o < nx:
                        lap2 = lap2 + F[o, pl.ds(r + PAD, n), :]
                x = src[j, pl.ds(r + PAD, n), :]
                for s in range(2):
                    if j == near[s]:
                        lap2 = lap2 + ghost[s] * x
                moved = src[j, pl.ds(r + (PAD + 1), n), :] - src[j, pl.ds(r + (PAD - 1), n), :]
                v = x + mobility(j, r, n) * F[j, pl.ds(r + PAD, n), :] - stiffness_step * lap2 + drift * moved
                dst[j, pl.ds(r + padded, n), :] = v
        rows(0, ny, update)

    def unpack(phase, s, lo, hi):
        def body(r, n):
            H[s, pl.ds(r + PAD, n), :] = RB[phase, s, 0, pl.ds(r, n), :].astype(F32)
        rows(lo, hi, body)

    def correct(phase, dst, padded, s, lo, hi):
        def body(r, n):
            h = H[s, pl.ds(r + PAD, n), :]
            v = dst[near[s], pl.ds(r + padded, n), :] + mobility(near[s], r, n) * h
            v = v - 2.0 * stiffness_step * in_plane(H, s, r, n) + RB[phase, s, 1, pl.ds(r, n), :].astype(F32)
            dst[near[s], pl.ds(r + padded, n), :] = v
            dst[far[s], pl.ds(r + padded, n), :] = dst[far[s], pl.ds(r + padded, n), :] - stiffness_step * h
        rows(lo, hi, body)

    def chosen(places):
        row = lax.broadcasted_iota(jnp.int32, (8, nz), 0)
        col = lax.broadcasted_iota(jnp.int32, (8, nz), 1)
        pick = jnp.zeros((8, nz), F32)
        for i, z in places:
            pick = jnp.where(jnp.logical_and(row == i, col == z), 1.0, pick)
        return pick

    def turned(pick, x, **kw):
        return lax.dot_general(pick, x, (((1,), (1,)), ((), ())), preferred_element_type=F32, **kw)

    pick_wall = chosen(((0, 0), (1, nz - 1)))
    pick_t = chosen(((0, 0), (1, nz - 1), (2, 1), (3, nz - 2))).astype(BF16)
    pick_q = chosen(((4, 0), (5, nz - 1))).astype(BF16)

    def wall_lanes(s):
        WS[s] = (turned(pick_t, SB[1, s, 0]) + turned(pick_q, SB[1, s, 1])).astype(BF16)

    def wall_out(s):
        return pltpu.make_async_remote_copy(
            src_ref=WS.at[s], dst_ref=WR.at[1 - s], send_sem=ws.at[s], recv_sem=wr.at[1 - s],
            device_id=(c, peer[s]), device_id_type=MESH,
        )

    def wall_in(s):
        return pltpu.make_async_remote_copy(
            src_ref=WS.at[1 - s], dst_ref=WR.at[s], send_sem=ws.at[1 - s], recv_sem=wr.at[s],
            device_id=(c, peer[s]), device_id_type=MESH,
        )

    ph_load.wait()
    local_step(S, S1, PAD)
    for k in range(CHUNKS):
        for s in range(2):
            @pl.when(has[s])
            def _():
                landing(0, s, k, *cuts[0][k]).wait_recv()
                unpack(0, s, *cuts[0][k])
                lo, hi = lagged(0, k, 16)
                correct(0, S1, PAD, s, lo, hi)
                split(S1, 1, s, lo, hi)
                residue(S1, 1, s, *cuts[1][k])
                if k < HELD:
                    piece(1, s, k, *cuts[1][k]).start()
                if k == CHUNKS - 1:
                    wall_lanes(s)
                    wall_out(s).start()
        if k == 1:
            send_own_half()

    def release(k):
        for s in range(2):
            @pl.when(has[s])
            def _():
                piece(1, s, k, *cuts[1][k]).start()

    @pl.when(jnp.logical_not(upper))
    def _():
        send_upper()

    for k in range(HELD, CHUNKS - 1):
        release(k)
    local_step(S1, OB, 0)

    lane_y = lax.broadcasted_iota(jnp.int32, (1, ny), 1)
    keep_first = (lane_y > 0).astype(F32)
    keep_last = (lane_y < ny - 1).astype(F32)
    for j in range(nx):
        both = S1[j, pl.ds(PAD, ny), :] + OB[j]
        BW[j] = turned(pick_wall, both, precision=lax.Precision.HIGHEST)[0:2, :]
        EP[j] = turned(pick_wall.astype(BF16), PB[j])[0:2, :]

    def wall_correct(s):
        w = WR[s].astype(F32)
        t, n, q = w[0:2, :], w[2:4, :], w[4:6, :]
        p = EP[near[s]]
        beside = pltpu.roll(t, 1, 1) * keep_first + pltpu.roll(t, ny - 1, 1) * keep_last
        d = ((3.0 * mobility_step) * (p * p) - mobility_step) * t + q
        d = d - 2.0 * stiffness_step * (n + beside - 6.0 * t)
        BW[near[s]] = BW[near[s]] + d
        BW[far[s]] = BW[far[s]] - stiffness_step * t

    def finish_chunk(k):
        lo, hi = lagged(1, k, 16)
        for s in range(2):
            @pl.when(has[s])
            def _():
                landing(1, s, k, *cuts[1][k]).wait_recv()
                unpack(1, s, *cuts[1][k])
                correct(1, OB, 0, s, lo, hi)

    n_red = GS.shape[0]
    stride = n_cond // n_red
    for s in range(2):
        @pl.when(has[s])
        def _():
            wall_in(s).wait_recv()
            wall_correct(s)
    for j in range(nx):
        p = EP[j]
        g = (1.0 - p * p) * BW[j]
        for w in range(2):
            GS[2 * j + w] = g[w : w + 1, :]

    @pl.when(c > 0)
    def _():
        pl.semaphore_wait(go2, 1)

    def part(r, slot):
        return pltpu.make_async_remote_copy(
            src_ref=GS.at[r], dst_ref=RR.at[slot], send_sem=gs.at[r], recv_sem=gr.at[slot],
            device_id=(r * stride, me), device_id_type=MESH,
        )

    def whole(d, r):
        return pltpu.make_async_remote_copy(
            src_ref=tot, dst_ref=FIN.at[r], send_sem=fs.at[d], recv_sem=fr.at[r],
            device_id=(d, me), device_id_type=MESH,
        )

    for r in range(n_red):
        @pl.when(c != r * stride)
        def _():
            part(r, c).start()

    mine_r = c // stride
    reducer = lax.rem(c, stride) == 0

    release(CHUNKS - 1)
    for k in range(CHUNKS - 2):
        finish_chunk(k)

    @pl.when(reducer)
    def _():
        tot[...] = GS[mine_r]

        def add(i, _):
            d = lax.rem(c + i, n_cond)
            part(mine_r, d).wait_recv()
            tot[...] = tot[...] + RR[d]
            return 0
        lax.fori_loop(1, n_cond, add, 0)

        def tell(i, _):
            whole(lax.rem(c + i, n_cond), mine_r).start()
            return 0
        lax.fori_loop(1, n_cond, tell, 0)
        FIN[mine_r] = tot[...]

    finish_chunk(CHUNKS - 2)

    def rows_in(i, _):
        d = lax.rem(me + i, n_slab)
        row_copy(d, d).wait_recv()
        return 0
    lax.fori_loop(1, n_slab, rows_in, 0)
    TA[...] = jnp.zeros_like(TA)
    for i in range(2):
        TA[pl.ds(i * n_slab, n_slab), pl.ds(0, nz)] = RT[:, i, :].astype(BF16)
    TA[:, pl.ds(nz, nz)] = jnp.ones((nz, nz), BF16)
    hi_sum = jnp.sum(RT[:, 2, :].astype(F32), axis=0, keepdims=True)
    lo_sum = jnp.sum(RT[:, 3, :].astype(F32), axis=0, keepdims=True)
    where_to = ((hi_sum - 1.0) * 16.0 + lo_sum).astype(jnp.int32)
    per = ny // nz
    for j in range(nx):
        for b in range(per):
            r = b * nz
            at = lax.broadcasted_iota(jnp.int32, (nz, nz), 0) + (j * ny + r)
            hit = (at == where_to).astype(F32).astype(BF16)
            both = jnp.dot(hit, TA[...], preferred_element_type=F32)
            p = PB[j, pl.ds(r, nz), :].astype(F32)
            OB[j, pl.ds(r, nz), :] = OB[j, pl.ds(r, nz), :] + (p * both[:, nz:] - both[:, :nz])


    finish_chunk(CHUNKS - 1)

    for r in range(n_red):
        @pl.when(c != r * stride)
        def _():
            whole(c, r).wait_recv()
    for w in range(2):
        for x in range(nx):
            grad[w, x : x + 1, :] = (wall_weight * mv[w, x : x + 1, :].astype(F32)) * FIN[2 * x + w]

    for phase in range(2):
        for s in range(2):
            @pl.when(has[s])
            def _():
                for k in range(CHUNKS):
                    piece(phase, s, k, *cuts[phase][k]).wait_send()

    def rows_out(i, _):
        d = lax.rem(me + i, n_slab)
        row_copy(d, me).wait_send()
        return 0
    lax.fori_loop(1, n_slab, rows_out, 0)
    for r in range(n_red):
        @pl.when(c != r * stride)
        def _():
            part(r, c).wait_send()

    @pl.when(reducer)
    def _():
        def sent(i, _):
            whole(lax.rem(c + i, n_cond), mine_r).wait_send()
            return 0
        lax.fori_loop(1, n_cond, sent, 0)
    for s in range(2):
        @pl.when(has[s])
        def _():
            wall_out(s).wait_send()


def deliver(state, walls, out, grad, sem):
    ny = state.shape[2]
    parts = [
        pltpu.make_async_copy(state.at[0, j], out.at[0, j], sem.at[j]) for j in range(state.shape[1])
    ]
    parts.append(pltpu.make_async_copy(walls, grad, sem.at[state.shape[1]]))
    for cp in parts:
        cp.start()
    for cp in parts:
        cp.wait()


def on_device(adjoint, phase, targets, owners, target_cell, rate_index, inflow_rates, wall_mask):
    n_cond = lax.axis_size("cond")
    n_slab = lax.axis_size("slab")
    _, nx, ny, nz = adjoint.shape
    n_rows = targets.shape[1]
    n_red = 2 * nx
    n_rates = inflow_rates.shape[0]
    hbm = pl.BlockSpec(memory_space=pltpu.HBM)
    vmem = pl.BlockSpec(memory_space=pltpu.VMEM)
    dma = pltpu.SemaphoreType.DMA
    padded = ny + 2 * PAD
    call = pl.pallas_call(
        functools.partial(kernel, n_cond, n_slab),
        out_shape=(
            pltpu.VMEM(adjoint.shape, F32),
            pltpu.VMEM(wall_mask.shape, F32),
        ),
        in_specs=[hbm] * 5 + [pl.BlockSpec(memory_space=pltpu.SMEM)] + [hbm] * 2,
        out_specs=(vmem, vmem),
        scratch_shapes=[
            pltpu.VMEM((nx, padded, nz), F32),
            pltpu.VMEM((nx, ny, nz), BF16),
            pltpu.VMEM((nx, padded, nz), F32),
            pltpu.VMEM((nx, padded, nz), F32),
            pltpu.VMEM((2, padded, nz), F32),
            pltpu.VMEM((2, padded, nz), F32),
            pltpu.VMEM((2, 2, 2, ny, nz), BF16),
            pltpu.VMEM((2, 2, 2, ny, nz), BF16),
            pltpu.VMEM((n_rows, nz), BF16),
            pltpu.VMEM((1, n_rows), jnp.int32),
            pltpu.VMEM((1, n_rows), jnp.int32),
            pltpu.VMEM(wall_mask.shape, jnp.int32),
            pltpu.VMEM((1, n_rates), F32),
            pltpu.VMEM((n_slab, 4, nz), ROW),
            pltpu.VMEM((n_slab, 4, nz), ROW),
            pltpu.VMEM((nz, 2 * nz), BF16),
            pltpu.VMEM((nx, 2, ny), F32),
            pltpu.VMEM((nx, 2, ny), F32),
            pltpu.VMEM((2, 8, ny), BF16),
            pltpu.VMEM((2, 8, ny), BF16),
            pltpu.VMEM((n_red, 1, ny), F32),
            pltpu.VMEM((n_cond, 1, ny), F32),
            pltpu.VMEM((n_red, 1, ny), F32),
            pltpu.VMEM((1, ny), F32),
            dma((nx + 6,)),
            dma((2, 2, CHUNKS)),
            dma((2, 2, CHUNKS)),
            dma((n_slab,)),
            dma((n_slab,)),
            dma((n_red,)),
            dma((n_cond,)),
            dma((n_cond,)),
            dma((n_red,)),
            dma((2,)),
            dma((2,)),
            pltpu.SemaphoreType.REGULAR,
            pltpu.SemaphoreType.REGULAR,
            pltpu.SemaphoreType.REGULAR,
        ],
        compiler_params=pltpu.CompilerParams(
            collective_id=0, has_side_effects=True, vmem_limit_bytes=56 * 1024 * 1024
        ),
    )
    owner_row = owners.reshape(1, n_rows)
    state, walls = call(
        adjoint, phase, targets, owner_row, target_cell,
        rate_index, inflow_rates.reshape(1, n_rates), wall_mask,
    )
    return pl.pallas_call(
        deliver,
        out_shape=(
            jax.ShapeDtypeStruct(adjoint.shape, F32),
            jax.ShapeDtypeStruct(wall_mask.shape, F32),
        ),
        in_specs=[pl.BlockSpec(memory_space=pl.ANY)] * 2,
        out_specs=(hbm, hbm),
        scratch_shapes=[dma((nx + 1,))],
        compiler_params=pltpu.CompilerParams(vmem_limit_bytes=4 * 1024 * 1024),
    )(state, walls)


ROW = BF16


def solution(mesh):
    in_specs = (
        P("cond", "slab", None, None),
        P("cond", "slab", None, None),
        P("cond", "slab", None),
        P("cond", "slab", None),
        P("cond", "slab"),
        P("cond"),
        P(),
        P(None, "slab", None),
    )
    out_specs = (P("cond", "slab", None, None), P(None, "slab", None))
    return jax.shard_map(
        on_device, mesh=mesh, in_specs=in_specs, out_specs=out_specs, check_vma=False
    )
```
